256 devices in a mesh: tm: 16 (over z_hi, y), chan: 16 (over z_lo, x, core).
Axes of the slice: x: 4, y: 4, z: 8 (z_hi: 4, z_lo: 2; z = z_hi * 2 + z_lo), core: 2. Of those that a mesh axis runs over, the one named last changes fastest.
Arguments:
- raw_data: bfloat16 [16384, 6144], P('chan', 'tm'), may hold values from -6 to 6
- band_taps: bfloat16 [61], replicated, may hold values from -0.75 to 0.75
- whitening: bfloat16 [16384, 1024], P('chan'), may hold values from -0.1875 to 0.1875
- band_offsets: int32 [128], P('chan'), may hold values from -3 to 3
- spatial: bfloat16 [1024, 3, 16384], P(None, None, 'chan'), may hold values from -0.0625 to 0.0625
- temporal: float32 [1024, 3, 61], replicated, may hold values from -0.4375 to 0.4375
Outputs:
- scores: float32 [1024, 6144], P('chan', 'tm')
The draws below stay inside these ranges and needn't reach their ends.
All inputs are finite; a program needn't handle non-finite values.
Results may differ from the reference program's by a relative error of at most 0.0041.
Values may be sent and summed in bfloat16 or wider, within the bound.
No kernel may reach another device: no remote copies, remote signals or barrier semaphores. Data moves between devices by JAX's collectives and lax.ppermute only.
A program may use at most 256 MiB of HBM per device.

```python
import jax
import jax.numpy as jnp
from jax import lax

C = 16384
PROBE_CH = 512
BAND = 1024
TILE = 128
K = 1024
R = 3
HALF = 30
TAPS = 61
SAMPLES = 6144
NPROBE = 32


def touch_ends(entries, own_key, least, high):
    longest = entries.shape.index(max(entries.shape))
    spots = []
    for shift in (0, 1):
        where = [jax.random.randint(jax.random.fold_in(own_key, axis), (), 0, length) for axis, length in enumerate(entries.shape)]
        where[longest] = (where[longest] + shift) % entries.shape[longest]
        spots.append(tuple(where))
    return entries.at[spots[0]].set(least).at[spots[1]].set(high)


def raised(entries, stream_key, source, target, blocks, factor):
    owner, partner = [(jnp.arange(entries.shape[dim]) // (entries.shape[dim] // blocks)).reshape([-1 if axis == dim else 1 for axis in range(entries.ndim)]) for dim in (source, target)]
    chosen = jax.random.permutation(stream_key, blocks)[partner]
    strong = (owner == chosen) | (owner == (partner + blocks // 2) % blocks)
    return jnp.where(strong, factor * entries, entries)


def levels(key, dims, shards, low, largest):
    factor_of = 1.0
    for axis_at, shards_of in shards:
        draws = jax.random.uniform(jax.random.fold_in(jax.random.fold_in(key, 6), axis_at), (shards_of,), jnp.float32, low / len(shards), largest / len(shards))
        factor_of = factor_of * jnp.repeat(jnp.exp(draws), dims[axis_at] // shards_of).reshape((-1,) + (1,) * (len(dims) - 1 - axis_at))
    return factor_of


def centred(stream_key, shape, spread, bound, pieces=(), kind=jnp.bfloat16):
    level = levels(stream_key, shape, pieces, -0.22, 0.18) if pieces else 1.0
    drawn = jax.random.normal(stream_key, shape, jnp.float32) * spread * level
    return jnp.minimum(jnp.maximum(drawn, -bound), bound).astype(kind)


def gaussian_with(key, shape, deviation, reach, cuts, heavy, held_as=jnp.bfloat16):
    entries = deviation * jax.random.normal(key, shape, jnp.float32)
    if cuts:
        entries = entries * levels(key, shape, cuts, -0.22, 0.18)
    return jnp.clip(raised(entries, jax.random.fold_in(key, 3), *heavy), -reach, reach).astype(held_as)


def setup_inputs(seed: int = 0) -> dict:
    splits = jax.random.split(jax.random.key(seed), 7)
    return {
        "raw_data": centred(splits[0], (C, SAMPLES), 1.0, 6.0, ((0, 16), (1, 16))),
        "band_taps": centred(splits[1], (TAPS,), TAPS ** -0.5, 0.75),
        "whitening": centred(splits[2], (C, BAND), BAND ** -0.5, 0.1875, ((0, 16),)),
        "band_offsets": touch_ends(jax.random.randint(splits[3], (C // TILE,), -3, 4), jax.random.fold_in(splits[3], 1), -3, 3).astype(jnp.int32),
        "spatial": gaussian_with(splits[4], (K, R, C), C ** -0.5, 0.0625, ((2, 16),), (2, 0, 16, 2.0)),
        "temporal": centred(splits[5], (K, R, TAPS), (R * TAPS) ** -0.5, 0.4375, (), jnp.float32),
    }


def band_filter(raw_data, band_taps):
    signal = raw_data.astype(jnp.float32)[:, None, :]
    kernel = band_taps.astype(jnp.float32)[None, None, :]
    result = lax.conv_general_dilated(signal, kernel, (1,), ((HALF, HALF),), dimension_numbers=("NCH", "OIH", "NCH"), precision=lax.Precision.HIGHEST)
    return result[:, 0, :].astype(jnp.bfloat16)


def whiten(filtered, whitening, band_offsets):
    groups = band_offsets.shape[0]

    def one_group(group_index):
        start_row = group_index * TILE + TILE // 2 - BAND // 2 + band_offsets[group_index] * TILE
        start_row = jnp.clip(start_row, 0, C - BAND).astype(jnp.int32)
        window = lax.dynamic_slice_in_dim(filtered, start_row, BAND, 0).astype(jnp.float32)
        weights = lax.dynamic_slice_in_dim(whitening, (group_index * TILE).astype(jnp.int32), TILE, 0).astype(jnp.float32)
        return jnp.dot(weights, window, precision=lax.Precision.HIGHEST)

    stacked = lax.map(one_group, jnp.arange(groups, dtype=jnp.int32))
    return stacked.reshape(C, filtered.shape[1]).astype(jnp.bfloat16)


def project(whitened, spatial):
    def one_block(summed, block_id):
        first_row = (block_id * PROBE_CH).astype(jnp.int32)
        block = lax.dynamic_slice_in_dim(whitened, first_row, PROBE_CH, 0).astype(jnp.float32)
        weights = lax.dynamic_slice_in_dim(spatial, first_row, PROBE_CH, 2).astype(jnp.float32)
        product = jnp.einsum("krc,cs->krs", weights, block, precision=lax.Precision.HIGHEST)
        return summed + product, None

    start_value = jnp.zeros((K, R, whitened.shape[1]), jnp.float32)
    summed, unused = lax.scan(one_block, start_value, jnp.arange(NPROBE, dtype=jnp.int32))
    return summed


def time_filter(projected, temporal):
    count = projected.shape[0]
    signal = projected.reshape(1, count * R, projected.shape[2])
    result = lax.conv_general_dilated(signal, temporal.astype(jnp.float32), (1,), ((HALF, HALF),), dimension_numbers=("NCH", "OIH", "NCH"), feature_group_count=count, precision=lax.Precision.HIGHEST)
    return result[0]


def reference(raw_data, band_taps, whitening, band_offsets, spatial, temporal):
    filtered = band_filter(raw_data, band_taps)
    whitened = whiten(filtered, whitening, band_offsets)
    projected = project(whitened, spatial)
    return time_filter(projected, temporal)
```

```python
import functools

import jax
import jax.numpy as jnp
import numpy as np
from jax import lax
from jax.experimental import pallas as pl
from jax.experimental.pallas import tpu as pltpu
from jax.sharding import PartitionSpec as P

LANES = 128
EDGE = 64
F = 256
POINTS = 2 * F - 1
WIDE = 512
REACH = 832


def halves(matrix):
    high = matrix.astype(jnp.bfloat16)
    low = (matrix - high.astype(np.float64)).astype(jnp.bfloat16)
    return high, low


def angles(samples):
    steps = np.outer(np.arange(samples), np.arange(F)) % POINTS
    return 2.0 * np.pi * steps / POINTS


def forward_matrix(samples, rows):
    turn = angles(samples)
    full = np.zeros((rows, 2 * F))
    full[:samples] = np.concatenate([np.cos(turn), np.sin(turn)], axis=1)
    return full


def inverse_matrix(samples):
    turn = angles(samples).T
    weight = np.full((F, 1), 2.0 / POINTS)
    weight[0] = 1.0 / POINTS
    return np.concatenate([weight * np.cos(turn), -weight * np.sin(turn)], axis=0)


def pack(edge):
    half = edge.shape[0] // 2
    return jnp.concatenate([edge[:half], edge[half:]], axis=1)


def rolled(row, rows, shift):
    wide = jnp.broadcast_to(row, (rows, row.shape[1]))
    return pltpu.roll(wide, shift % row.shape[1], 1, stride=1, stride_axis=0)


def filter_kernel(taps, samples, span_ref, raw_ref, prev_ref, next_ref, row_ref, own_ref, up_ref, down_ref, toep_ref):
    rows = raw_ref.shape[0]
    half = rows // 2
    row = row_ref[...]
    reach = (taps - 1) // 8 * 8
    column = lax.broadcasted_iota(jnp.int32, (1, WIDE), 1)
    keep = (column >= span_ref[0]) & (column < span_ref[1])
    toep_ref[:samples] = jnp.where(keep, rolled(row, samples, reach), 0.0).astype(jnp.bfloat16)
    toep_ref[samples : samples + EDGE] = jnp.where(keep, rolled(row, EDGE, reach - EDGE), 0.0).astype(jnp.bfloat16)
    toep_ref[samples + EDGE :] = jnp.where(keep, rolled(row, EDGE, reach + samples), 0.0).astype(jnp.bfloat16)

    lane = lax.broadcasted_iota(jnp.int32, (half, LANES), 1)
    prev = prev_ref[...].astype(jnp.float32)
    after = next_ref[...].astype(jnp.float32)
    low = lane < EDGE
    sides = (
        jnp.where(low, prev, pltpu.roll(after, EDGE, 1)).astype(jnp.bfloat16),
        jnp.where(low, pltpu.roll(prev, EDGE, 1), after).astype(jnp.bfloat16),
    )
    for part in range(2):
        body = slice(part * half, (part + 1) * half)
        value = jnp.dot(raw_ref[body], toep_ref[:samples], preferred_element_type=jnp.float32)
        value += jnp.dot(sides[part], toep_ref[samples:], preferred_element_type=jnp.float32)
        own_ref[body] = value.astype(jnp.bfloat16)
    whole = samples // LANES
    fold = REACH // 2
    for ref, begin in ((up_ref, rows - REACH), (down_ref, 0)):
        for block in range(whole):
            ref[block * REACH : (block + 1) * REACH] = own_ref[begin : begin + REACH, block * LANES : (block + 1) * LANES]
        first = own_ref[begin : begin + fold, samples:].astype(jnp.float32)
        second = own_ref[begin + fold : begin + REACH, samples:].astype(jnp.float32)
        ref[whole * REACH :] = (first + pltpu.roll(second, EDGE, 1)).astype(jnp.bfloat16)


def score_kernel(groups, samples, meta_ref, own_ref, before_ref, after_ref, white_ref, fh_ref, fl_ref, ih_ref, il_ref, spatial_ref, hat_ref, keep_ref, send_ref, ext_ref, what_ref):
    rows = own_ref.shape[0]
    tile = rows // groups
    band = white_ref.shape[1]

    @pl.when(pl.program_id(0) == 0)
    def _():
        whole = samples // LANES
        fold = REACH // 2
        low = lax.broadcasted_iota(jnp.int32, (fold, LANES), 1) < EDGE
        ext_ref[REACH : REACH + rows] = own_ref[...]
        for ref, begin in ((before_ref, 0), (after_ref, REACH + rows)):
            for block in range(whole):
                ext_ref[begin : begin + REACH, block * LANES : (block + 1) * LANES] = ref[block * REACH : (block + 1) * REACH]
            last = ref[whole * REACH :].astype(jnp.float32)
            ext_ref[begin : begin + fold, samples:] = jnp.where(low, last, 0.0).astype(jnp.bfloat16)
            ext_ref[begin + fold : begin + REACH, samples:] = jnp.where(low, pltpu.roll(last, EDGE, 1), 0.0).astype(jnp.bfloat16)
        for group in range(groups):
            start = pl.multiple_of(meta_ref[group], EDGE)
            body = slice(group * tile, (group + 1) * tile)
            value = jnp.dot(white_ref[body], ext_ref[pl.ds(start, band)], preferred_element_type=jnp.float32)
            value = value.astype(jnp.bfloat16)
            hat = jnp.dot(value, fh_ref[...], preferred_element_type=jnp.float32)
            hat += jnp.dot(value, fl_ref[...], preferred_element_type=jnp.float32)
            what_ref[body] = hat.astype(jnp.bfloat16)

    rank, block, _ = spatial_ref.shape
    weights = spatial_ref[...].reshape(rank * block, rows)
    product = jnp.dot(weights, what_ref[...], preferred_element_type=jnp.float32)
    real = imag = 0.0
    for r in range(rank):
        a = product[r * block : (r + 1) * block, :F]
        b = product[r * block : (r + 1) * block, F:]
        c = hat_ref[r, :, :F]
        d = hat_ref[r, :, F:]
        real += a * c + b * d
        imag += a * d - b * c
    real = real.astype(jnp.bfloat16)
    imag = imag.astype(jnp.bfloat16)
    value = jnp.dot(real, ih_ref[:F], preferred_element_type=jnp.float32)
    value += jnp.dot(real, il_ref[:F], preferred_element_type=jnp.float32)
    value += jnp.dot(imag, ih_ref[F:], preferred_element_type=jnp.float32)
    value += jnp.dot(imag, il_ref[F:], preferred_element_type=jnp.float32)
    own = keep_ref.shape[1]
    core = meta_ref[groups]
    for pair in range(block // (2 * own)):
        even = value[2 * pair * own : (2 * pair + 1) * own]
        odd = value[(2 * pair + 1) * own : (2 * pair + 2) * own]
        keep_ref[pair] = jnp.where(core == 0, even, odd)
        send_ref[pair] = jnp.where(core == 0, odd, even).astype(jnp.bfloat16)


def local(raw, band_taps, whitening, band_offsets, spatial, temporal):
    rows, samples = raw.shape
    taps = band_taps.shape[0]
    groups = band_offsets.shape[0]
    tile = rows // groups
    band = whitening.shape[1]
    templates, rank, _ = spatial.shape
    half_taps = taps // 2
    window = samples + taps - 1
    n_tm = lax.axis_size("tm")
    n_chan = lax.axis_size("chan")
    t = lax.axis_index("tm")
    c = lax.axis_index("chan")
    own = templates // n_chan

    up = [(i, i + 1) for i in range(n_tm - 1)]
    down = [(j, i) for i, j in up]
    prev = lax.ppermute(pack(raw[:, samples - EDGE :]), "tm", up)
    after = lax.ppermute(pack(raw[:, :EDGE]), "tm", down)

    reverse = band_taps.astype(jnp.float32)
    row = jnp.concatenate([reverse[:1], jnp.zeros((WIDE - taps,), jnp.float32), reverse[1:][::-1]])
    row = jnp.roll(row, (taps - 1) % 8)[None]
    begin = jnp.where(t == 0, half_taps, 0)
    end = jnp.where(t == n_tm - 1, samples + half_taps, window)
    span = jnp.stack([begin, end]).astype(jnp.int32)
    payload = (samples // LANES) * REACH + REACH // 2
    vmem = pl.BlockSpec(memory_space=pltpu.VMEM)
    smem = pl.BlockSpec(memory_space=pltpu.SMEM)
    filtered, to_up, to_down = pl.pallas_call(
        functools.partial(filter_kernel, taps, samples),
        out_shape=(
            jax.ShapeDtypeStruct((rows, WIDE), jnp.bfloat16),
            jax.ShapeDtypeStruct((payload, LANES), jnp.bfloat16),
            jax.ShapeDtypeStruct((payload, LANES), jnp.bfloat16),
        ),
        in_specs=[smem, vmem, vmem, vmem, vmem],
        out_specs=(vmem, vmem, vmem),
        scratch_shapes=[pltpu.VMEM((WIDE, WIDE), jnp.bfloat16)],
        compiler_params=pltpu.CompilerParams(vmem_limit_bytes=24 << 20),
        name="filter",
    )(span, raw, prev, after, row)

    up = [(i, i + 1) for i in range(n_chan - 1)]
    down = [(j, i) for i, j in up]
    before_rows = lax.ppermute(to_up, "chan", up)
    after_rows = lax.ppermute(to_down, "chan", down)

    hat = jnp.einsum(
        "krj,jf->rkf",
        temporal,
        jnp.asarray(forward_matrix(taps, taps), jnp.float32),
        precision=lax.Precision.HIGHEST,
    )
    first_row = c * rows
    row_begin = first_row + jnp.arange(groups, dtype=jnp.int32) * tile
    start = row_begin + tile // 2 - band // 2 + band_offsets * tile
    start = jnp.clip(start, 0, n_chan * rows - band) - first_row + REACH
    start = jnp.clip(start, 0, 2 * REACH + rows - band)
    meta = jnp.concatenate([start, (c % 2)[None]]).astype(jnp.int32)

    fh, fl = (jnp.asarray(m) for m in halves(forward_matrix(window, WIDE)))
    ih, il = (jnp.asarray(m) for m in halves(inverse_matrix(samples)))
    block = 256
    pairs = block // (2 * own)

    def fixed(shape):
        return pl.BlockSpec(shape, lambda i, m: (0,) * len(shape), pipeline_mode=pl.Buffered(1))

    keep, send = pl.pallas_call(
        functools.partial(score_kernel, groups, samples),
        out_shape=(
            jax.ShapeDtypeStruct((n_chan // 2, own, samples), jnp.float32),
            jax.ShapeDtypeStruct((n_chan // 2, own, samples), jnp.bfloat16),
        ),
        grid_spec=pltpu.PrefetchScalarGridSpec(
            num_scalar_prefetch=1,
            grid=(templates // block,),
            in_specs=[
                fixed((rows, WIDE)),
                fixed((payload, LANES)),
                fixed((payload, LANES)),
                fixed((rows, band)),
                fixed(fh.shape),
                fixed(fl.shape),
                fixed(ih.shape),
                fixed(il.shape),
                pl.BlockSpec((rank, block, rows), lambda i, m: (0, i, 0)),
                pl.BlockSpec((rank, block, 2 * F), lambda i, m: (0, i, 0)),
            ],
            out_specs=(
                pl.BlockSpec((pairs, own, samples), lambda i, m: (i, 0, 0)),
                pl.BlockSpec((pairs, own, samples), lambda i, m: (i, 0, 0)),
            ),
            scratch_shapes=[
                pltpu.VMEM((2 * REACH + rows, WIDE), jnp.bfloat16),
                pltpu.VMEM((rows, 2 * F), jnp.bfloat16),
            ],
        ),
        compiler_params=pltpu.CompilerParams(vmem_limit_bytes=40 << 20),
        name="score",
    )(meta, filtered, before_rows, after_rows, whitening, fh, fl, ih, il, spatial.transpose(1, 0, 2), hat)

    other = lax.ppermute(send, "chan", [(i, i ^ 1) for i in range(n_chan)])
    both = (keep + other.astype(jnp.float32)).astype(jnp.bfloat16)
    members = [[2 * i + core for i in range(n_chan // 2)] for core in range(2)]
    shares = lax.all_to_all(both, "chan", 0, 0, axis_index_groups=members)
    return jnp.sum(shares.astype(jnp.float32), axis=0)


def solution(mesh):
    placed = (P("chan", "tm"), P(), P("chan", None), P("chan"), P(None, None, "chan"), P())
    return jax.shard_map(local, mesh=mesh, in_specs=placed, out_specs=P("chan", "tm"), check_vma=False)
```

```python
import functools

import jax
import jax.numpy as jnp
import numpy as np
from jax import lax
from jax.experimental import pallas as pl
from jax.experimental.pallas import tpu as pltpu
from jax.sharding import PartitionSpec as P

LANES = 128
EDGE = 64
F = 256
POINTS = 2 * F - 1
WIDE = 512
REACH = 832


def halves(matrix):
    high = matrix.astype(jnp.bfloat16)
    low = (matrix - high.astype(np.float64)).astype(jnp.bfloat16)
    return np.stack([high, low])


def angles(samples):
    steps = np.outer(np.arange(samples), np.arange(F)) % POINTS
    return 2.0 * np.pi * steps / POINTS


def forward_matrix(samples, rows):
    turn = angles(samples)
    full = np.zeros((rows, 2 * F))
    full[:samples] = np.concatenate([np.cos(turn), np.sin(turn)], axis=1)
    return full


def inverse_matrix(samples):
    turn = angles(samples).T
    weight = np.full((F, 1), 2.0 / POINTS)
    weight[0] = 1.0 / POINTS
    return np.concatenate([weight * np.cos(turn), -weight * np.sin(turn)], axis=0)


def pack(edge):
    half = edge.shape[0] // 2
    return jnp.concatenate([edge[:half], edge[half:]], axis=1)


def rolled(row, rows, shift):
    wide = jnp.broadcast_to(row, (rows, row.shape[1]))
    return pltpu.roll(wide, shift % row.shape[1], 1, stride=1, stride_axis=0)


def toeplitz_kernel(samples, taps_ref, toep_ref):
    taps = taps_ref.shape[1]
    t = lax.axis_index("tm")
    last = lax.axis_size("tm") - 1
    rest = (taps - 1) % 8
    reach = taps - 1 - rest
    tap = lax.broadcasted_iota(jnp.int32, (taps, WIDE), 0)
    lane = lax.broadcasted_iota(jnp.int32, (taps, WIDE), 1)
    place = (lane == rest - tap) | (lane == rest - tap + WIDE)
    picked = jnp.broadcast_to(taps_ref[...], (8, taps))
    row = jnp.dot(picked, place.astype(jnp.bfloat16), preferred_element_type=jnp.float32)[:1]
    begin = jnp.where(t == 0, taps // 2, 0)
    end = samples + jnp.where(t == last, taps // 2, taps - 1)
    column = lax.broadcasted_iota(jnp.int32, (1, WIDE), 1)
    keep = (column >= begin) & (column < end)
    toep_ref[:samples] = jnp.where(keep, rolled(row, samples, reach), 0.0).astype(jnp.bfloat16)
    toep_ref[samples : samples + EDGE] = jnp.where(keep, rolled(row, EDGE, reach - EDGE), 0.0).astype(jnp.bfloat16)
    toep_ref[samples + EDGE :] = jnp.where(keep, rolled(row, EDGE, reach + samples), 0.0).astype(jnp.bfloat16)


def score_kernel(
    chunks,
    offsets_ref,
    toep_ref,
    sides_ref,
    before_ref,
    before_sides_ref,
    after_ref,
    after_sides_ref,
    raw_hbm,
    white_hbm,
    forward_hbm,
    inverse_hbm,
    spatial_hbm,
    hat_hbm,
    keep_ref,
    send_ref,
    raw_ref,
    white_ref,
    forward_ref,
    inverse_ref,
    spatial_ref,
    hat_ref,
    wide_ref,
    filtered_ref,
    what_ref,
    raw_sem,
    white_sem,
    forward_sem,
    inverse_sem,
    spatial_sem,
    hat_sem,
):
    rows, samples = raw_ref.shape
    groups = offsets_ref.shape[0]
    tile = rows // groups
    band = white_ref.shape[1]
    c = lax.axis_index("chan")
    all_rows = lax.axis_size("chan") * rows
    rank, templates, _ = spatial_ref.shape
    block = templates // chunks

    first = [
        pltpu.make_async_copy(raw_hbm, raw_ref, raw_sem),
        pltpu.make_async_copy(white_hbm, white_ref, white_sem),
        pltpu.make_async_copy(forward_hbm, forward_ref, forward_sem),
    ]
    for copy in first:
        copy.start()
    later = []
    for chunk in range(chunks):
        part = (slice(None), slice(chunk * block, (chunk + 1) * block))
        later.append(
            (
                pltpu.make_async_copy(spatial_hbm.at[part], spatial_ref.at[part], spatial_sem.at[chunk]),
                pltpu.make_async_copy(hat_hbm.at[part], hat_ref.at[part], hat_sem.at[chunk]),
            )
        )
        later[-1][0].start()
        later[-1][1].start()
        if chunk == 0:
            last = pltpu.make_async_copy(inverse_hbm, inverse_ref, inverse_sem)
            last.start()

    def filter_rows(main, sides, begin):
        count = main.shape[0]
        wide_ref[begin : begin + count, :samples] = main[...]
        wide_ref[begin : begin + count, samples:] = sides[...]
        value = jnp.dot(wide_ref[begin : begin + count], toep_ref[...], preferred_element_type=jnp.float32)
        filtered_ref[begin : begin + count] = value.astype(jnp.bfloat16)

    first[0].wait()
    filter_rows(raw_ref, sides_ref, REACH)
    filter_rows(before_ref.at[rows - REACH :], before_sides_ref, 0)
    filter_rows(after_ref.at[:REACH], after_sides_ref, REACH + rows)

    first[1].wait()
    first[2].wait()
    for group in range(groups):
        begin = c * rows + group * tile
        start = begin + tile // 2 - band // 2 + offsets_ref[group] * tile
        start = jnp.clip(start, 0, all_rows - band) - c * rows + REACH
        start = pl.multiple_of(jnp.clip(start, 0, 2 * REACH + rows - band), EDGE)
        body = slice(group * tile, (group + 1) * tile)
        value = jnp.dot(white_ref[body], filtered_ref[pl.ds(start, band)], preferred_element_type=jnp.float32)
        value = value.astype(jnp.bfloat16)
        hat = jnp.dot(value, forward_ref[0], preferred_element_type=jnp.float32)
        hat += jnp.dot(value, forward_ref[1], preferred_element_type=jnp.float32)
        what_ref[body] = hat.astype(jnp.bfloat16)

    own = keep_ref.shape[1]
    even_core = c % 2 == 0
    last.wait()
    for chunk in range(chunks):
        later[chunk][0].wait()
        later[chunk][1].wait()
        body = slice(chunk * block, (chunk + 1) * block)
        weights = spatial_ref[:, body].reshape(rank * block, rows)
        product = jnp.dot(weights, what_ref[...], preferred_element_type=jnp.float32)
        real = imag = 0.0
        for r in range(rank):
            a = product[r * block : (r + 1) * block, :F]
            b = product[r * block : (r + 1) * block, F:]
            x = hat_ref[r, body, :F]
            y = hat_ref[r, body, F:]
            real += a * x + b * y
            imag += a * y - b * x
        both = jnp.concatenate([real, imag], axis=1).astype(jnp.bfloat16)
        value = jnp.dot(both, inverse_ref[0], preferred_element_type=jnp.float32)
        value += jnp.dot(both, inverse_ref[1], preferred_element_type=jnp.float32)
        pairs = block // (2 * own)
        for pair in range(pairs):
            even = value[2 * pair * own : (2 * pair + 1) * own]
            odd = value[(2 * pair + 1) * own : (2 * pair + 2) * own]
            keep_ref[chunk * pairs + pair] = jnp.where(even_core, even, odd)
            send_ref[chunk * pairs + pair] = jnp.where(even_core, odd, even).astype(jnp.bfloat16)


def local(raw, band_taps, whitening, band_offsets, spatial, temporal):
    rows, samples = raw.shape
    taps = band_taps.shape[0]
    band = whitening.shape[1]
    templates, rank, _ = spatial.shape
    window = samples + taps - 1
    n_tm = lax.axis_size("tm")
    n_chan = lax.axis_size("chan")
    own = templates // n_chan
    half = rows // 2
    chunks = 4

    up = [(i, i + 1) for i in range(n_chan - 1)]
    down = [(j, i) for i, j in up]
    up_tm = [(i, i + 1) for i in range(n_tm - 1)]
    down_tm = [(j, i) for i, j in up_tm]
    before = lax.ppermute(raw, "chan", up)
    after = lax.ppermute(raw, "chan", down)
    prev = lax.ppermute(pack(raw[:, samples - EDGE :]), "tm", up_tm)
    follow = lax.ppermute(pack(raw[:, :EDGE]), "tm", down_tm)
    sides = jnp.concatenate(
        [
            jnp.concatenate([prev[:, :EDGE], follow[:, :EDGE]], axis=1),
            jnp.concatenate([prev[:, EDGE:], follow[:, EDGE:]], axis=1),
        ],
        axis=0,
    )
    before_sides = lax.ppermute(sides[rows - REACH :], "chan", up)
    after_sides = lax.ppermute(sides[:REACH], "chan", down)

    vmem = pl.BlockSpec(memory_space=pltpu.VMEM)
    smem = pl.BlockSpec(memory_space=pltpu.SMEM)
    hbm = pl.BlockSpec(memory_space=pltpu.MemorySpace.HBM)
    toep = pl.pallas_call(
        functools.partial(toeplitz_kernel, samples),
        out_shape=jax.ShapeDtypeStruct((WIDE, WIDE), jnp.bfloat16),
        in_specs=[vmem],
        out_specs=vmem,
        cost_estimate=pl.CostEstimate(flops=WIDE * WIDE * 64, bytes_accessed=WIDE * WIDE * 4, transcendentals=0),
        compiler_params=pltpu.CompilerParams(vmem_limit_bytes=8 << 20),
        name="toeplitz",
    )(band_taps[None])
    hat = jnp.einsum(
        "krj,jf->rkf",
        temporal,
        jnp.asarray(forward_matrix(taps, taps), jnp.float32),
        precision=lax.Precision.HIGH,
    )
    forward = jnp.asarray(halves(forward_matrix(window, WIDE)))
    inverse = jnp.asarray(halves(inverse_matrix(samples)))

    out_shape = (n_chan // 2, own, samples)
    work = 2 * (2 * REACH + rows) * WIDE * WIDE + 2 * rows * WIDE * (band + 2 * WIDE) + 2 * templates * WIDE * (rank * rows + 2 * samples)
    keep, send = pl.pallas_call(
        functools.partial(score_kernel, chunks),
        out_shape=(
            jax.ShapeDtypeStruct(out_shape, jnp.float32),
            jax.ShapeDtypeStruct(out_shape, jnp.bfloat16),
        ),
        in_specs=[smem] + [vmem] * 6 + [hbm] * 6,
        out_specs=(vmem, vmem),
        scratch_shapes=[
            pltpu.VMEM((rows, samples), jnp.bfloat16),
            pltpu.VMEM((rows, band), jnp.bfloat16),
            pltpu.VMEM(forward.shape, jnp.bfloat16),
            pltpu.VMEM(inverse.shape, jnp.bfloat16),
            pltpu.VMEM((rank, templates, rows), jnp.bfloat16),
            pltpu.VMEM((rank, templates, 2 * F), jnp.float32),
            pltpu.VMEM((2 * REACH + rows, WIDE), jnp.bfloat16),
            pltpu.VMEM((2 * REACH + rows, WIDE), jnp.bfloat16),
            pltpu.VMEM((rows, 2 * F), jnp.bfloat16),
            pltpu.SemaphoreType.DMA,
            pltpu.SemaphoreType.DMA,
            pltpu.SemaphoreType.DMA,
            pltpu.SemaphoreType.DMA,
            pltpu.SemaphoreType.DMA((chunks,)),
            pltpu.SemaphoreType.DMA((chunks,)),
        ],
        cost_estimate=pl.CostEstimate(flops=work, bytes_accessed=24 << 20, transcendentals=0),
        compiler_params=pltpu.CompilerParams(vmem_limit_bytes=44 << 20),
        name="score",
    )(band_offsets, toep, sides, before, before_sides, after, after_sides, raw, whitening, forward, inverse, spatial.transpose(1, 0, 2), hat)

    other = lax.ppermute(send, "chan", [(i, i ^ 1) for i in range(n_chan)])
    both = (keep + other.astype(jnp.float32)).astype(jnp.bfloat16)
    members = [[2 * i + core for i in range(n_chan // 2)] for core in range(2)]
    shares = lax.all_to_all(both, "chan", 0, 0, axis_index_groups=members)
    return jnp.sum(shares.astype(jnp.float32), axis=0)


def solution(mesh):
    placed = (P("chan", "tm"), P(), P("chan", None), P("chan"), P(None, None, "chan"), P())
    return jax.shard_map(local, mesh=mesh, in_specs=placed, out_specs=P("chan", "tm"), check_vma=False)
```

```python
import functools

import jax
import jax.numpy as jnp
import numpy as np
from jax import lax
from jax.experimental import pallas as pl
from jax.experimental.pallas import tpu as pltpu
from jax.sharding import PartitionSpec as P

LANES = 128
EDGE = 64
F = 256
POINTS = 2 * F - 1
WIDE = 512
REACH = 832


def halves(matrix):
    high = matrix.astype(jnp.bfloat16)
    low = (matrix - high.astype(np.float64)).astype(jnp.bfloat16)
    return np.stack([high, low])


def angles(samples):
    steps = np.outer(np.arange(samples), np.arange(F)) % POINTS
    return 2.0 * np.pi * steps / POINTS


def forward_matrix(samples, rows):
    turn = angles(samples)
    full = np.zeros((rows, 2 * F))
    full[:samples] = np.concatenate([np.cos(turn), np.sin(turn)], axis=1)
    return full


def inverse_matrix(samples, reach):
    place = np.concatenate([np.arange(samples + EDGE), np.arange(-EDGE, 0)])
    used = (place >= -reach) & (place < samples + reach)
    turn = 2.0 * np.pi * (np.outer(np.arange(F), place) % POINTS) / POINTS
    weight = np.full((F, 1), 2.0 / POINTS)
    weight[0] = 1.0 / POINTS
    return np.concatenate([weight * np.cos(turn), -weight * np.sin(turn)], axis=0) * used


def rolled(row, rows, shift):
    wide = jnp.broadcast_to(row, (rows, row.shape[1]))
    return pltpu.roll(wide, shift % row.shape[1], 1, stride=1, stride_axis=0)


def toeplitz_kernel(samples, taps_ref, toep_ref):
    taps = taps_ref.shape[1]
    t = lax.axis_index("tm")
    last = lax.axis_size("tm") - 1
    rest = (taps - 1) % 8
    reach = taps - 1 - rest
    tap = lax.broadcasted_iota(jnp.int32, (taps, WIDE), 0)
    lane = lax.broadcasted_iota(jnp.int32, (taps, WIDE), 1)
    place = (lane == rest - tap) | (lane == rest - tap + WIDE)
    picked = jnp.broadcast_to(taps_ref[...], (8, taps))
    row = jnp.dot(picked, place.astype(jnp.bfloat16), preferred_element_type=jnp.float32)[:1]
    begin = jnp.where(t == 0, taps // 2, 0)
    end = samples + jnp.where(t == last, taps // 2, taps - 1)
    column = lax.broadcasted_iota(jnp.int32, (1, WIDE), 1)
    keep = (column >= begin) & (column < end)
    toep_ref[...] = jnp.where(keep, rolled(row, samples, reach), 0.0).astype(jnp.bfloat16)


def score_kernel(
    chunks,
    offsets_ref,
    toep_ref,
    before_ref,
    after_ref,
    raw_hbm,
    white_hbm,
    forward_hbm,
    inverse_hbm,
    spatial_hbm,
    hat_hbm,
    keep_ref,
    send_ref,
    raw_ref,
    white_ref,
    forward_ref,
    inverse_ref,
    spatial_ref,
    hat_ref,
    filtered_ref,
    what_ref,
    raw_sem,
    white_sem,
    forward_sem,
    inverse_sem,
    spatial_sem,
    hat_sem,
):
    rows, samples = raw_ref.shape
    groups = offsets_ref.shape[0]
    tile = rows // groups
    band = white_ref.shape[1]
    c = lax.axis_index("chan")
    all_rows = lax.axis_size("chan") * rows
    rank, templates, _ = spatial_ref.shape
    block = templates // chunks

    first = [
        pltpu.make_async_copy(raw_hbm, raw_ref, raw_sem),
        pltpu.make_async_copy(white_hbm, white_ref, white_sem),
        pltpu.make_async_copy(forward_hbm, forward_ref, forward_sem),
    ]
    for copy in first:
        copy.start()
    later = []
    for chunk in range(chunks):
        part = (slice(None), slice(chunk * block, (chunk + 1) * block))
        later.append(
            (
                pltpu.make_async_copy(spatial_hbm.at[part], spatial_ref.at[part], spatial_sem.at[chunk]),
                pltpu.make_async_copy(hat_hbm.at[part], hat_ref.at[part], hat_sem.at[chunk]),
            )
        )
        later[-1][0].start()
        later[-1][1].start()
        if chunk == 0:
            last = pltpu.make_async_copy(inverse_hbm, inverse_ref, inverse_sem)
            last.start()

    def filter_rows(main, begin):
        value = jnp.dot(main[...], toep_ref[...], preferred_element_type=jnp.float32)
        filtered_ref[begin : begin + main.shape[0]] = value.astype(jnp.bfloat16)

    first[0].wait()
    filter_rows(raw_ref, REACH)
    filter_rows(before_ref, 0)
    filter_rows(after_ref, REACH + rows)

    first[1].wait()
    first[2].wait()
    for group in range(groups):
        begin = c * rows + group * tile
        start = begin + tile // 2 - band // 2 + offsets_ref[group] * tile
        start = jnp.clip(start, 0, all_rows - band) - c * rows + REACH
        start = pl.multiple_of(jnp.clip(start, 0, 2 * REACH + rows - band), EDGE)
        body = slice(group * tile, (group + 1) * tile)
        value = jnp.dot(white_ref[body], filtered_ref[pl.ds(start, band)], preferred_element_type=jnp.float32)
        value = value.astype(jnp.bfloat16)
        hat = jnp.dot(value, forward_ref[0], preferred_element_type=jnp.float32)
        hat += jnp.dot(value, forward_ref[1], preferred_element_type=jnp.float32)
        what_ref[body] = hat.astype(jnp.bfloat16)

    own = keep_ref.shape[1]
    even_core = c % 2 == 0
    last.wait()
    for chunk in range(chunks):
        later[chunk][0].wait()
        later[chunk][1].wait()
        body = slice(chunk * block, (chunk + 1) * block)
        weights = spatial_ref[:, body].reshape(rank * block, rows)
        product = jnp.dot(weights, what_ref[...], preferred_element_type=jnp.float32)
        real = imag = 0.0
        for r in range(rank):
            a = product[r * block : (r + 1) * block, :F]
            b = product[r * block : (r + 1) * block, F:]
            x = hat_ref[r, body, :F]
            y = hat_ref[r, body, F:]
            real += a * x + b * y
            imag += a * y - b * x
        both = jnp.concatenate([real, imag], axis=1).astype(jnp.bfloat16)
        value = jnp.dot(both, inverse_ref[0], preferred_element_type=jnp.float32)
        value += jnp.dot(both, inverse_ref[1], preferred_element_type=jnp.float32)
        pairs = block // (2 * own)
        for pair in range(pairs):
            even = value[2 * pair * own : (2 * pair + 1) * own]
            odd = value[(2 * pair + 1) * own : (2 * pair + 2) * own]
            keep_ref[chunk * pairs + pair] = jnp.where(even_core, even, odd)
            send_ref[chunk * pairs + pair] = jnp.where(even_core, odd, even).astype(jnp.bfloat16)


def local(raw, band_taps, whitening, band_offsets, spatial, temporal):
    rows, samples = raw.shape
    taps = band_taps.shape[0]
    band = whitening.shape[1]
    templates, rank, _ = spatial.shape
    window = samples + taps - 1
    n_tm = lax.axis_size("tm")
    n_chan = lax.axis_size("chan")
    own = templates // n_chan
    chunks = 4

    up = [(i, i + 1) for i in range(n_chan - 1)]
    down = [(j, i) for i, j in up]
    before = lax.ppermute(raw[rows - REACH :], "chan", up)
    after = lax.ppermute(raw[:REACH], "chan", down)

    vmem = pl.BlockSpec(memory_space=pltpu.VMEM)
    smem = pl.BlockSpec(memory_space=pltpu.SMEM)
    hbm = pl.BlockSpec(memory_space=pltpu.MemorySpace.HBM)
    toep = pl.pallas_call(
        functools.partial(toeplitz_kernel, samples),
        out_shape=jax.ShapeDtypeStruct((samples, WIDE), jnp.bfloat16),
        in_specs=[vmem],
        out_specs=vmem,
        cost_estimate=pl.CostEstimate(flops=WIDE * WIDE * 64, bytes_accessed=WIDE * WIDE * 4, transcendentals=0),
        compiler_params=pltpu.CompilerParams(vmem_limit_bytes=8 << 20),
        name="toeplitz",
    )(band_taps[None])
    hat = jnp.einsum(
        "krj,jf->rkf",
        temporal,
        jnp.asarray(forward_matrix(taps, taps), jnp.float32),
        precision=lax.Precision.HIGH,
    )
    forward = jnp.asarray(halves(forward_matrix(window, WIDE)))
    inverse = jnp.asarray(halves(inverse_matrix(samples, taps - 1)))

    out_shape = (n_chan // 2, own, WIDE)
    work = 2 * (2 * REACH + rows) * WIDE * samples + 2 * rows * WIDE * (band + 2 * WIDE) + 2 * templates * WIDE * (rank * rows + 2 * WIDE)
    keep, send = pl.pallas_call(
        functools.partial(score_kernel, chunks),
        out_shape=(
            jax.ShapeDtypeStruct(out_shape, jnp.float32),
            jax.ShapeDtypeStruct(out_shape, jnp.bfloat16),
        ),
        in_specs=[smem] + [vmem] * 3 + [hbm] * 6,
        out_specs=(vmem, vmem),
        scratch_shapes=[
            pltpu.VMEM((rows, samples), jnp.bfloat16),
            pltpu.VMEM((rows, band), jnp.bfloat16),
            pltpu.VMEM(forward.shape, jnp.bfloat16),
            pltpu.VMEM(inverse.shape, jnp.bfloat16),
            pltpu.VMEM((rank, templates, rows), jnp.bfloat16),
            pltpu.VMEM((rank, templates, 2 * F), jnp.float32),
            pltpu.VMEM((2 * REACH + rows, WIDE), jnp.bfloat16),
            pltpu.VMEM((rows, 2 * F), jnp.bfloat16),
            pltpu.SemaphoreType.DMA,
            pltpu.SemaphoreType.DMA,
            pltpu.SemaphoreType.DMA,
            pltpu.SemaphoreType.DMA,
            pltpu.SemaphoreType.DMA((chunks,)),
            pltpu.SemaphoreType.DMA((chunks,)),
        ],
        cost_estimate=pl.CostEstimate(flops=work, bytes_accessed=24 << 20, transcendentals=0),
        compiler_params=pltpu.CompilerParams(vmem_limit_bytes=44 << 20),
        name="score",
    )(band_offsets, toep, before, after, raw, whitening, forward, inverse, spatial.transpose(1, 0, 2), hat)

    other = lax.ppermute(send, "chan", [(i, i ^ 1) for i in range(n_chan)])
    total = keep + other.astype(jnp.float32)
    edges = total[..., samples:].astype(jnp.bfloat16)
    up_tm = [(i, i + 1) for i in range(n_tm - 1)]
    down_tm = [(j, i) for i, j in up_tm]
    prev = lax.ppermute(edges, "tm", up_tm).astype(jnp.float32)
    follow = lax.ppermute(edges, "tm", down_tm).astype(jnp.float32)
    low = lax.broadcasted_iota(jnp.int32, (1, 1, LANES), 2) < EDGE
    both = jnp.concatenate(
        [
            total[..., :LANES] + jnp.where(low, prev, 0.0),
            total[..., LANES : samples - LANES],
            total[..., samples - LANES : samples] + jnp.where(low, 0.0, follow),
        ],
        axis=-1,
    ).astype(jnp.bfloat16)
    members = [[2 * i + core for i in range(n_chan // 2)] for core in range(2)]
    shares = lax.all_to_all(both, "chan", 0, 0, axis_index_groups=members)
    return jnp.sum(shares.astype(jnp.float32), axis=0)


def solution(mesh):
    placed = (P("chan", "tm"), P(), P("chan", None), P("chan"), P(None, None, "chan"), P())
    return jax.shard_map(local, mesh=mesh, in_specs=placed, out_specs=P("chan", "tm"), check_vma=False)
```

```python
import functools

import jax
import jax.numpy as jnp
import numpy as np
from jax import lax
from jax.experimental import pallas as pl
from jax.experimental.pallas import tpu as pltpu
from jax.sharding import PartitionSpec as P

LANES = 128
EDGE = 64
F = 256
POINTS = 2 * F - 1
WIDE = 512
SLOT = 64
REACH = 832


def halves(matrix):
    high = matrix.astype(jnp.bfloat16)
    low = (matrix - high.astype(np.float64)).astype(jnp.bfloat16)
    return np.stack([high, low])


def angles(samples):
    steps = np.outer(np.arange(samples), np.arange(F)) % POINTS
    return 2.0 * np.pi * steps / POINTS


def split_matrix(taps):
    high, low = halves(forward_matrix(taps, SLOT))
    return np.concatenate([high, low, high])


def forward_matrix(samples, rows):
    turn = angles(samples)
    full = np.zeros((rows, 2 * F))
    full[:samples] = np.concatenate([np.cos(turn), np.sin(turn)], axis=1)
    return full


def inverse_matrix(samples):
    turn = angles(samples).T
    weight = np.full((F, 1), 2.0 / POINTS)
    weight[0] = 1.0 / POINTS
    return np.concatenate([weight * np.cos(turn), -weight * np.sin(turn)], axis=0)


def pack(edge):
    half = edge.shape[0] // 2
    return jnp.concatenate([edge[:half], edge[half:]], axis=1)


def rolled(row, rows, shift):
    wide = jnp.broadcast_to(row, (rows, row.shape[1]))
    return pltpu.roll(wide, shift % row.shape[1], 1, stride=1, stride_axis=0)


def prepare_kernel(samples, taps_ref, temporal_ref, toep_ref, split_ref):
    rank, count, templates = temporal_ref.shape
    blank = jnp.zeros((SLOT - count, templates), jnp.float32)
    for r in range(rank):
        value = jnp.concatenate([temporal_ref[r], blank], axis=0)
        high = value.astype(jnp.bfloat16).astype(jnp.float32)
        stacked = jnp.concatenate([high, high, value - high], axis=0)
        split_ref[r] = stacked.T.astype(jnp.bfloat16)
    taps = taps_ref.shape[1]
    t = lax.axis_index("tm")
    last = lax.axis_size("tm") - 1
    rest = (taps - 1) % 8
    reach = taps - 1 - rest
    tap = lax.broadcasted_iota(jnp.int32, (taps, WIDE), 0)
    lane = lax.broadcasted_iota(jnp.int32, (taps, WIDE), 1)
    place = (lane == rest - tap) | (lane == rest - tap + WIDE)
    picked = jnp.broadcast_to(taps_ref[...], (8, taps))
    row = jnp.dot(picked, place.astype(jnp.bfloat16), preferred_element_type=jnp.float32)[:1]
    begin = jnp.where(t == 0, taps // 2, 0)
    end = samples + jnp.where(t == last, taps // 2, taps - 1)
    column = lax.broadcasted_iota(jnp.int32, (1, WIDE), 1)
    keep = (column >= begin) & (column < end)
    toep_ref[:samples] = jnp.where(keep, rolled(row, samples, reach), 0.0).astype(jnp.bfloat16)
    toep_ref[samples : samples + EDGE] = jnp.where(keep, rolled(row, EDGE, reach - EDGE), 0.0).astype(jnp.bfloat16)
    toep_ref[samples + EDGE :] = jnp.where(keep, rolled(row, EDGE, reach + samples), 0.0).astype(jnp.bfloat16)


def score_kernel(
    chunks,
    offsets_ref,
    toep_ref,
    sides_ref,
    before_ref,
    before_sides_ref,
    after_ref,
    after_sides_ref,
    split_ref,
    spread_ref,
    raw_hbm,
    white_hbm,
    forward_hbm,
    inverse_hbm,
    spatial_hbm,
    keep_ref,
    send_ref,
    raw_ref,
    white_ref,
    forward_ref,
    inverse_ref,
    spatial_ref,
    wide_ref,
    filtered_ref,
    what_ref,
    raw_sem,
    white_sem,
    forward_sem,
    inverse_sem,
    spatial_sem,
):
    rows, samples = raw_ref.shape
    groups = offsets_ref.shape[0]
    tile = rows // groups
    band = white_ref.shape[1]
    c = lax.axis_index("chan")
    all_rows = lax.axis_size("chan") * rows
    rank, templates, _ = spatial_ref.shape
    block = templates // chunks

    first = [
        pltpu.make_async_copy(raw_hbm, raw_ref, raw_sem),
        pltpu.make_async_copy(white_hbm, white_ref, white_sem),
        pltpu.make_async_copy(forward_hbm, forward_ref, forward_sem),
    ]
    for copy in first:
        copy.start()
    later = []
    for chunk in range(chunks):
        part = (slice(None), slice(chunk * block, (chunk + 1) * block))
        later.append(pltpu.make_async_copy(spatial_hbm.at[part], spatial_ref.at[part], spatial_sem.at[chunk]))
        later[-1].start()
        if chunk == 0:
            last = pltpu.make_async_copy(inverse_hbm, inverse_ref, inverse_sem)
            last.start()

    def filter_rows(main, sides, begin):
        count = main.shape[0]
        wide_ref[begin : begin + count, :samples] = main[...]
        wide_ref[begin : begin + count, samples:] = sides[...]
        value = jnp.dot(wide_ref[begin : begin + count], toep_ref[...], preferred_element_type=jnp.float32)
        filtered_ref[begin : begin + count] = value.astype(jnp.bfloat16)

    first[0].wait()
    filter_rows(raw_ref, sides_ref, REACH)
    filter_rows(before_ref, before_sides_ref, 0)
    filter_rows(after_ref, after_sides_ref, REACH + rows)

    first[1].wait()
    first[2].wait()
    for group in range(groups):
        begin = c * rows + group * tile
        start = begin + tile // 2 - band // 2 + offsets_ref[group] * tile
        start = jnp.clip(start, 0, all_rows - band) - c * rows + REACH
        start = pl.multiple_of(jnp.clip(start, 0, 2 * REACH + rows - band), EDGE)
        body = slice(group * tile, (group + 1) * tile)
        value = jnp.dot(white_ref[body], filtered_ref[pl.ds(start, band)], preferred_element_type=jnp.float32)
        value = value.astype(jnp.bfloat16)
        hat = jnp.dot(value, forward_ref[0], preferred_element_type=jnp.float32)
        hat += jnp.dot(value, forward_ref[1], preferred_element_type=jnp.float32)
        what_ref[body] = hat.astype(jnp.bfloat16)

    own = keep_ref.shape[1]
    even_core = c % 2 == 0
    last.wait()
    for chunk in range(chunks):
        later[chunk].wait()
        body = slice(chunk * block, (chunk + 1) * block)
        weights = spatial_ref[:, body].reshape(rank * block, rows)
        product = jnp.dot(weights, what_ref[...], preferred_element_type=jnp.float32)
        split = split_ref[:, body].reshape(rank * block, split_ref.shape[2])
        hat = jnp.dot(split, spread_ref[...], preferred_element_type=jnp.float32)
        real = imag = 0.0
        for r in range(rank):
            a = product[r * block : (r + 1) * block, :F]
            b = product[r * block : (r + 1) * block, F:]
            x = hat[r * block : (r + 1) * block, :F]
            y = hat[r * block : (r + 1) * block, F:]
            real += a * x + b * y
            imag += a * y - b * x
        both = jnp.concatenate([real, imag], axis=1).astype(jnp.bfloat16)
        value = jnp.dot(both, inverse_ref[0], preferred_element_type=jnp.float32)
        value += jnp.dot(both, inverse_ref[1], preferred_element_type=jnp.float32)
        pairs = block // (2 * own)
        for pair in range(pairs):
            even = value[2 * pair * own : (2 * pair + 1) * own]
            odd = value[(2 * pair + 1) * own : (2 * pair + 2) * own]
            keep_ref[chunk * pairs + pair] = jnp.where(even_core, even, odd)
            send_ref[chunk * pairs + pair] = jnp.where(even_core, odd, even).astype(jnp.bfloat16)


def local(raw, band_taps, whitening, band_offsets, spatial, temporal):
    rows, samples = raw.shape
    taps = band_taps.shape[0]
    band = whitening.shape[1]
    templates, rank, _ = spatial.shape
    window = samples + taps - 1
    n_tm = lax.axis_size("tm")
    n_chan = lax.axis_size("chan")
    own = templates // n_chan
    half = rows // 2
    chunks = 4

    up = [(i, i + 1) for i in range(n_chan - 1)]
    down = [(j, i) for i, j in up]
    up_tm = [(i, i + 1) for i in range(n_tm - 1)]
    down_tm = [(j, i) for i, j in up_tm]
    before = lax.ppermute(raw[rows - REACH :], "chan", up)
    after = lax.ppermute(raw[:REACH], "chan", down)
    prev = lax.ppermute(pack(raw[:, samples - EDGE :]), "tm", up_tm)
    follow = lax.ppermute(pack(raw[:, :EDGE]), "tm", down_tm)
    sides = jnp.concatenate(
        [
            jnp.concatenate([prev[:, :EDGE], follow[:, :EDGE]], axis=1),
            jnp.concatenate([prev[:, EDGE:], follow[:, EDGE:]], axis=1),
        ],
        axis=0,
    )
    before_sides = lax.ppermute(sides[rows - REACH :], "chan", up)
    after_sides = lax.ppermute(sides[:REACH], "chan", down)

    vmem = pl.BlockSpec(memory_space=pltpu.VMEM)
    smem = pl.BlockSpec(memory_space=pltpu.SMEM)
    hbm = pl.BlockSpec(memory_space=pltpu.MemorySpace.HBM)
    toep, split = pl.pallas_call(
        functools.partial(prepare_kernel, samples),
        out_shape=(
            jax.ShapeDtypeStruct((WIDE, WIDE), jnp.bfloat16),
            jax.ShapeDtypeStruct((rank, templates, 3 * SLOT), jnp.bfloat16),
        ),
        in_specs=[vmem, vmem],
        out_specs=(vmem, vmem),
        cost_estimate=pl.CostEstimate(flops=WIDE * WIDE * 64, bytes_accessed=4 << 20, transcendentals=0),
        compiler_params=pltpu.CompilerParams(vmem_limit_bytes=12 << 20),
        name="prepare",
    )(band_taps[None], temporal.transpose(1, 2, 0))
    spread = jnp.asarray(split_matrix(taps))
    forward = jnp.asarray(halves(forward_matrix(window, WIDE)))
    inverse = jnp.asarray(halves(inverse_matrix(samples)))

    out_shape = (n_chan // 2, own, samples)
    work = 2 * (2 * REACH + rows) * WIDE * WIDE + 2 * rows * WIDE * (band + 2 * WIDE) + 2 * templates * WIDE * (rank * (rows + 3 * SLOT) + 2 * samples)
    keep, send = pl.pallas_call(
        functools.partial(score_kernel, chunks),
        out_shape=(
            jax.ShapeDtypeStruct(out_shape, jnp.float32),
            jax.ShapeDtypeStruct(out_shape, jnp.bfloat16),
        ),
        in_specs=[smem] + [vmem] * 8 + [hbm] * 5,
        out_specs=(vmem, vmem),
        scratch_shapes=[
            pltpu.VMEM((rows, samples), jnp.bfloat16),
            pltpu.VMEM((rows, band), jnp.bfloat16),
            pltpu.VMEM(forward.shape, jnp.bfloat16),
            pltpu.VMEM(inverse.shape, jnp.bfloat16),
            pltpu.VMEM((rank, templates, rows), jnp.bfloat16),
            pltpu.VMEM((2 * REACH + rows, WIDE), jnp.bfloat16),
            pltpu.VMEM((2 * REACH + rows, WIDE), jnp.bfloat16),
            pltpu.VMEM((rows, 2 * F), jnp.bfloat16),
            pltpu.SemaphoreType.DMA,
            pltpu.SemaphoreType.DMA,
            pltpu.SemaphoreType.DMA,
            pltpu.SemaphoreType.DMA,
            pltpu.SemaphoreType.DMA((chunks,)),
        ],
        cost_estimate=pl.CostEstimate(flops=work, bytes_accessed=16 << 20, transcendentals=0),
        compiler_params=pltpu.CompilerParams(vmem_limit_bytes=40 << 20),
        name="score",
    )(band_offsets, toep, sides, before, before_sides, after, after_sides, split, spread, raw, whitening, forward, inverse, spatial.transpose(1, 0, 2))

    other = lax.ppermute(send, "chan", [(i, i ^ 1) for i in range(n_chan)])
    both = (keep + other.astype(jnp.float32)).astype(jnp.bfloat16)
    members = [[2 * i + core for i in range(n_chan // 2)] for core in range(2)]
    shares = lax.all_to_all(both, "chan", 0, 0, axis_index_groups=members)
    return jnp.sum(shares.astype(jnp.float32), axis=0)


def solution(mesh):
    placed = (P("chan", "tm"), P(), P("chan", None), P("chan"), P(None, None, "chan"), P())
    return jax.shard_map(local, mesh=mesh, in_specs=placed, out_specs=P("chan", "tm"), check_vma=False)
```

```python
import functools

import jax
import jax.numpy as jnp
import numpy as np
from jax import lax
from jax.experimental import pallas as pl
from jax.experimental.pallas import tpu as pltpu
from jax.sharding import PartitionSpec as P

LANES = 128
EDGE = 64
F = 256
POINTS = 2 * F - 1
WIDE = 512
SLOT = 64
REACH = 832


def halves(matrix):
    high = matrix.astype(jnp.bfloat16)
    low = (matrix - high.astype(np.float64)).astype(jnp.bfloat16)
    return np.stack([high, low])


def angles(samples):
    steps = np.outer(np.arange(samples), np.arange(F)) % POINTS
    return 2.0 * np.pi * steps / POINTS


def split_matrix(taps):
    high, low = halves(forward_matrix(taps, SLOT))
    return np.concatenate([high, low, high])


def forward_matrix(samples, rows):
    turn = angles(samples)
    full = np.zeros((rows, 2 * F))
    full[:samples] = np.concatenate([np.cos(turn), np.sin(turn)], axis=1)
    return full


def inverse_matrix(samples):
    turn = angles(samples).T
    weight = np.full((F, 1), 2.0 / POINTS)
    weight[0] = 1.0 / POINTS
    return np.concatenate([weight * np.cos(turn), -weight * np.sin(turn)], axis=0)


def pack(edge):
    half = edge.shape[0] // 2
    return jnp.concatenate([edge[:half], edge[half:]], axis=1)


def rolled(row, rows, shift):
    wide = jnp.broadcast_to(row, (rows, row.shape[1]))
    return pltpu.roll(wide, shift % row.shape[1], 1, stride=1, stride_axis=0)


def early_kernel(samples, taps_ref, temporal_ref, spread_ref, raw_ref, sides_ref, mate_ref, mate_sides_ref, toep_ref, hat_ref, own_ref, near_ref, wide_ref):
    taps = taps_ref.shape[1]
    t = lax.axis_index("tm")
    last = lax.axis_size("tm") - 1
    rest = (taps - 1) % 8
    reach = taps - 1 - rest
    tap = lax.broadcasted_iota(jnp.int32, (taps, WIDE), 0)
    lane = lax.broadcasted_iota(jnp.int32, (taps, WIDE), 1)
    place = (lane == rest - tap) | (lane == rest - tap + WIDE)
    picked = jnp.broadcast_to(taps_ref[...], (8, taps))
    row = jnp.dot(picked, place.astype(jnp.bfloat16), preferred_element_type=jnp.float32)[:1]
    begin = jnp.where(t == 0, taps // 2, 0)
    end = samples + jnp.where(t == last, taps // 2, taps - 1)
    column = lax.broadcasted_iota(jnp.int32, (1, WIDE), 1)
    keep = (column >= begin) & (column < end)
    prev = rolled(row, EDGE, reach - EDGE)
    follow = rolled(row, EDGE, reach + samples)
    even = t % 2 == 0
    toep_ref[:samples] = jnp.where(keep, rolled(row, samples, reach), 0.0).astype(jnp.bfloat16)
    toep_ref[samples : samples + EDGE] = jnp.where(keep, jnp.where(even, follow, prev), 0.0).astype(jnp.bfloat16)
    toep_ref[samples + EDGE :] = jnp.where(keep, jnp.where(even, prev, follow), 0.0).astype(jnp.bfloat16)

    rank, count, templates = temporal_ref.shape
    blank = jnp.zeros((SLOT - count, templates), jnp.float32)
    for r in range(rank):
        value = jnp.concatenate([temporal_ref[r], blank], axis=0)
        high = value.astype(jnp.bfloat16).astype(jnp.float32)
        stacked = jnp.concatenate([high, high, value - high], axis=0)
        hat_ref[r] = jnp.dot(stacked.T.astype(jnp.bfloat16), spread_ref[...], preferred_element_type=jnp.float32)

    for main, sides, out in ((raw_ref, sides_ref, own_ref), (mate_ref, mate_sides_ref, near_ref)):
        count = main.shape[0]
        wide_ref[:count, :samples] = main[...]
        wide_ref[:count, samples:] = sides[...]
        out[...] = jnp.dot(wide_ref[:count], toep_ref[...], preferred_element_type=jnp.float32).astype(jnp.bfloat16)


def score_kernel(
    chunks,
    offsets_ref,
    toep_ref,
    far_ref,
    far_sides_ref,
    hat_ref,
    own_hbm,
    near_hbm,
    white_hbm,
    forward_hbm,
    inverse_hbm,
    spatial_hbm,
    keep_ref,
    send_ref,
    white_ref,
    forward_ref,
    inverse_ref,
    spatial_ref,
    wide_ref,
    filtered_ref,
    whitened_ref,
    what_ref,
    own_sem,
    near_sem,
    white_sem,
    forward_sem,
    inverse_sem,
    spatial_sem,
):
    rows, band = white_ref.shape
    samples = far_ref.shape[1]
    groups = offsets_ref.shape[0]
    tile = rows // groups
    c = lax.axis_index("chan")
    all_rows = lax.axis_size("chan") * rows
    rank, templates, _ = spatial_ref.shape
    block = templates // chunks
    even_core = c % 2 == 0
    near = pl.multiple_of(jnp.where(even_core, REACH + rows, 0), EDGE)
    far = pl.multiple_of(jnp.where(even_core, 0, REACH + rows), EDGE)

    own_copy = pltpu.make_async_copy(own_hbm, filtered_ref.at[REACH : REACH + rows], own_sem)
    near_copy = pltpu.make_async_copy(near_hbm, filtered_ref.at[pl.ds(near, REACH)], near_sem)
    white_copy = pltpu.make_async_copy(white_hbm, white_ref, white_sem)
    forward_copy = pltpu.make_async_copy(forward_hbm, forward_ref, forward_sem)
    inverse_copy = pltpu.make_async_copy(inverse_hbm, inverse_ref, inverse_sem)
    for copy in (own_copy, near_copy, white_copy, forward_copy):
        copy.start()
    later = []
    for chunk in range(chunks):
        part = (slice(None), slice(chunk * block, (chunk + 1) * block))
        later.append(pltpu.make_async_copy(spatial_hbm.at[part], spatial_ref.at[part], spatial_sem.at[chunk]))
        later[-1].start()
        if chunk == 0:
            inverse_copy.start()

    wide_ref[:, :samples] = far_ref[...]
    wide_ref[:, samples:] = far_sides_ref[...]
    value = jnp.dot(wide_ref[...], toep_ref[...], preferred_element_type=jnp.float32)
    filtered_ref[pl.ds(far, REACH)] = value.astype(jnp.bfloat16)

    own_copy.wait()
    near_copy.wait()
    white_copy.wait()
    for group in range(groups):
        begin = c * rows + group * tile
        start = begin + tile // 2 - band // 2 + offsets_ref[group] * tile
        start = jnp.clip(start, 0, all_rows - band) - c * rows + REACH
        start = pl.multiple_of(jnp.clip(start, 0, 2 * REACH + rows - band), EDGE)
        body = slice(group * tile, (group + 1) * tile)
        value = jnp.dot(white_ref[body], filtered_ref[pl.ds(start, band)], preferred_element_type=jnp.float32)
        whitened_ref[body] = value.astype(jnp.bfloat16)
    forward_copy.wait()
    value = jnp.dot(whitened_ref[...], forward_ref[0], preferred_element_type=jnp.float32)
    value += jnp.dot(whitened_ref[...], forward_ref[1], preferred_element_type=jnp.float32)
    what_ref[...] = value.astype(jnp.bfloat16)

    own = keep_ref.shape[1]
    inverse_copy.wait()
    for chunk in range(chunks):
        later[chunk].wait()
        body = slice(chunk * block, (chunk + 1) * block)
        weights = spatial_ref[:, body].reshape(rank * block, rows)
        product = jnp.dot(weights, what_ref[...], preferred_element_type=jnp.float32)
        real = imag = 0.0
        for r in range(rank):
            a = product[r * block : (r + 1) * block, :F]
            b = product[r * block : (r + 1) * block, F:]
            x = hat_ref[r, body, :F]
            y = hat_ref[r, body, F:]
            real += a * x + b * y
            imag += a * y - b * x
        both = jnp.concatenate([real, imag], axis=1).astype(jnp.bfloat16)
        value = jnp.dot(both, inverse_ref[0], preferred_element_type=jnp.float32)
        value += jnp.dot(both, inverse_ref[1], preferred_element_type=jnp.float32)
        pairs = block // (2 * own)
        for pair in range(pairs):
            even = value[2 * pair * own : (2 * pair + 1) * own]
            odd = value[(2 * pair + 1) * own : (2 * pair + 2) * own]
            keep_ref[chunk * pairs + pair] = jnp.where(even_core, even, odd)
            send_ref[chunk * pairs + pair] = jnp.where(even_core, odd, even).astype(jnp.bfloat16)


def couples(size):
    first = [(i, i ^ 1) for i in range(size)]
    second = [(i, ((i + 1) ^ 1) - 1) for i in range(1, size - 1)]
    return first, second


def local(raw, band_taps, whitening, band_offsets, spatial, temporal):
    rows, samples = raw.shape
    taps = band_taps.shape[0]
    band = whitening.shape[1]
    templates, rank, _ = spatial.shape
    window = samples + taps - 1
    n_tm = lax.axis_size("tm")
    n_chan = lax.axis_size("chan")
    own = templates // n_chan
    chunks = 2

    near_chan, far_chan = couples(n_chan)
    near_tm, far_tm = couples(n_tm)
    even_tm = lax.axis_index("tm") % 2 == 0
    even_chan = lax.axis_index("chan") % 2 == 0

    def facing(array):
        upper, lower = array[rows - REACH :], array[:REACH]
        return jnp.where(even_chan, upper, lower), jnp.where(even_chan, lower, upper)

    ahead, behind = pack(raw[:, samples - EDGE :]), pack(raw[:, :EDGE])
    first = lax.ppermute(jnp.where(even_tm, ahead, behind), "tm", near_tm)
    second = lax.ppermute(jnp.where(even_tm, behind, ahead), "tm", far_tm)
    to_near, to_far = facing(raw)
    near = lax.ppermute(to_near, "chan", near_chan)
    far = lax.ppermute(to_far, "chan", far_chan)
    sides = jnp.concatenate(
        [
            jnp.concatenate([first[:, :EDGE], second[:, :EDGE]], axis=1),
            jnp.concatenate([first[:, EDGE:], second[:, EDGE:]], axis=1),
        ],
        axis=0,
    )
    to_near, to_far = facing(sides)
    far_sides = lax.ppermute(to_far, "chan", far_chan)
    near_sides = lax.ppermute(to_near, "chan", near_chan)

    vmem = pl.BlockSpec(memory_space=pltpu.VMEM)
    smem = pl.BlockSpec(memory_space=pltpu.SMEM)
    hbm = pl.BlockSpec(memory_space=pl.ANY)
    bf16 = jnp.bfloat16
    early = 2 * (rows + REACH) * WIDE * WIDE + 2 * rank * templates * 3 * SLOT * 2 * F
    toep, hat, own_rows, near_rows = pl.pallas_call(
        functools.partial(early_kernel, samples),
        out_shape=(
            jax.ShapeDtypeStruct((WIDE, WIDE), bf16),
            jax.ShapeDtypeStruct((rank, templates, 2 * F), jnp.float32),
            jax.ShapeDtypeStruct((rows, WIDE), bf16),
            jax.ShapeDtypeStruct((REACH, WIDE), bf16),
        ),
        in_specs=[vmem] * 7,
        out_specs=(vmem,) * 4,
        scratch_shapes=[pltpu.VMEM((rows, WIDE), bf16)],
        cost_estimate=pl.CostEstimate(flops=early, bytes_accessed=12 << 20, transcendentals=0),
        compiler_params=pltpu.CompilerParams(vmem_limit_bytes=24 << 20),
        name="early",
    )(band_taps[None], temporal.transpose(1, 2, 0), jnp.asarray(split_matrix(taps)), raw, sides, near, near_sides)
    forward = jnp.asarray(halves(forward_matrix(window, WIDE)))
    inverse = jnp.asarray(halves(inverse_matrix(samples)))

    out_shape = (n_chan // 2, own, samples)
    work = 2 * REACH * WIDE * WIDE + 2 * rows * WIDE * (band + 2 * WIDE) + 2 * templates * WIDE * (rank * rows + 2 * samples)
    keep, send = pl.pallas_call(
        functools.partial(score_kernel, chunks),
        out_shape=(
            jax.ShapeDtypeStruct(out_shape, jnp.float32),
            jax.ShapeDtypeStruct(out_shape, bf16),
        ),
        in_specs=[smem] + [vmem] * 4 + [hbm] * 6,
        out_specs=(vmem, vmem),
        scratch_shapes=[
            pltpu.VMEM((rows, band), bf16),
            pltpu.VMEM(forward.shape, bf16),
            pltpu.VMEM(inverse.shape, bf16),
            pltpu.VMEM((rank, templates, rows), bf16),
            pltpu.VMEM((REACH, WIDE), bf16),
            pltpu.VMEM((2 * REACH + rows, WIDE), bf16),
            pltpu.VMEM((rows, WIDE), bf16),
            pltpu.VMEM((rows, 2 * F), bf16),
            pltpu.SemaphoreType.DMA,
            pltpu.SemaphoreType.DMA,
            pltpu.SemaphoreType.DMA,
            pltpu.SemaphoreType.DMA,
            pltpu.SemaphoreType.DMA,
            pltpu.SemaphoreType.DMA((chunks,)),
        ],
        cost_estimate=pl.CostEstimate(flops=work, bytes_accessed=16 << 20, transcendentals=0),
        compiler_params=pltpu.CompilerParams(vmem_limit_bytes=36 << 20),
        name="score",
    )(band_offsets, toep, far, far_sides, hat, own_rows, near_rows, whitening, forward, inverse, spatial.transpose(1, 0, 2))

    other = lax.ppermute(send, "chan", near_chan)
    both = (keep + other.astype(jnp.float32)).astype(bf16)
    members = [[2 * i + core for i in range(n_chan // 2)] for core in range(2)]
    shares = lax.all_to_all(both, "chan", 0, 0, axis_index_groups=members)
    return jnp.sum(shares.astype(jnp.float32), axis=0)


def solution(mesh):
    placed = (P("chan", "tm"), P(), P("chan", None), P("chan"), P(None, None, "chan"), P())
    return jax.shard_map(local, mesh=mesh, in_specs=placed, out_specs=P("chan", "tm"), check_vma=False)
```

```python
import functools

import jax
import jax.numpy as jnp
import numpy as np
from jax import lax
from jax.experimental import pallas as pl
from jax.experimental.pallas import tpu as pltpu
from jax.sharding import PartitionSpec as P

LANES = 128
EDGE = 64
F = 256
POINTS = 2 * F - 1
WIDE = 512
SLOT = 64
REACH = 832


def halves(matrix):
    high = matrix.astype(jnp.bfloat16)
    low = (matrix - high.astype(np.float64)).astype(jnp.bfloat16)
    return np.stack([high, low])


def angles(samples):
    steps = np.outer(np.arange(samples), np.arange(F)) % POINTS
    return 2.0 * np.pi * steps / POINTS


def split_matrix(taps):
    high, low = halves(forward_matrix(taps, SLOT))
    return np.concatenate([high, low, high])


def forward_matrix(samples, rows):
    turn = angles(samples)
    full = np.zeros((rows, 2 * F))
    full[:samples] = np.concatenate([np.cos(turn), np.sin(turn)], axis=1)
    return full


def inverse_matrix(samples):
    turn = angles(samples).T
    weight = np.full((F, 1), 2.0 / POINTS)
    weight[0] = 1.0 / POINTS
    return np.concatenate([weight * np.cos(turn), -weight * np.sin(turn)], axis=0)


def pack_kernel(raw_hbm, near_ref, far_ref, edge_ref, edge_sem):
    rows, samples = raw_hbm.shape
    half = rows // 2
    copies = [
        pltpu.make_async_copy(raw_hbm.at[:, begin : begin + LANES], edge_ref.at[part], edge_sem.at[part])
        for part, begin in enumerate((0, samples - LANES))
    ]
    for copy in copies:
        copy.start()
    low = lax.broadcasted_iota(jnp.int32, (half, LANES), 1) < EDGE
    even = lax.axis_index("tm") % 2 == 0
    for copy in copies:
        copy.wait()
    first = edge_ref[0].astype(jnp.float32)
    last = edge_ref[1].astype(jnp.float32)
    behind = jnp.where(low, first[:half], pltpu.roll(first[half:], EDGE, 1)).astype(jnp.bfloat16)
    ahead = jnp.where(low, pltpu.roll(last[:half], EDGE, 1), last[half:]).astype(jnp.bfloat16)
    near_ref[...] = jnp.where(even, ahead, behind)
    far_ref[...] = jnp.where(even, behind, ahead)


def face_kernel(raw_hbm, near_ref, far_ref, near_sem, far_sem):
    rows = raw_hbm.shape[0]
    even = lax.axis_index("chan") % 2 == 0
    upper, lower = rows - REACH, 0
    copies = []
    for ref, sem, begin in ((far_ref, far_sem, jnp.where(even, lower, upper)), (near_ref, near_sem, jnp.where(even, upper, lower))):
        part = pl.ds(pl.multiple_of(begin, EDGE), REACH)
        copies.append(pltpu.make_async_copy(raw_hbm.at[part], ref, sem))
        copies[-1].start()
    for copy in copies:
        copy.wait()


def rolled(row, rows, shift):
    wide = jnp.broadcast_to(row, (rows, row.shape[1]))
    return pltpu.roll(wide, shift % row.shape[1], 1, stride=1, stride_axis=0)


def early_kernel(samples, taps_ref, temporal_ref, spread_ref, raw_ref, sides_ref, mate_ref, mate_sides_ref, toep_ref, hat_ref, own_ref, near_ref, wide_ref):
    taps = taps_ref.shape[1]
    t = lax.axis_index("tm")
    last = lax.axis_size("tm") - 1
    rest = (taps - 1) % 8
    reach = taps - 1 - rest
    tap = lax.broadcasted_iota(jnp.int32, (taps, WIDE), 0)
    lane = lax.broadcasted_iota(jnp.int32, (taps, WIDE), 1)
    place = (lane == rest - tap) | (lane == rest - tap + WIDE)
    picked = jnp.broadcast_to(taps_ref[...], (8, taps))
    row = jnp.dot(picked, place.astype(jnp.bfloat16), preferred_element_type=jnp.float32)[:1]
    begin = jnp.where(t == 0, taps // 2, 0)
    end = samples + jnp.where(t == last, taps // 2, taps - 1)
    column = lax.broadcasted_iota(jnp.int32, (1, WIDE), 1)
    keep = (column >= begin) & (column < end)
    prev = rolled(row, EDGE, reach - EDGE)
    follow = rolled(row, EDGE, reach + samples)
    even = t % 2 == 0
    toep_ref[:samples] = jnp.where(keep, rolled(row, samples, reach), 0.0).astype(jnp.bfloat16)
    toep_ref[samples : samples + EDGE] = jnp.where(keep, jnp.where(even, follow, prev), 0.0).astype(jnp.bfloat16)
    toep_ref[samples + EDGE :] = jnp.where(keep, jnp.where(even, prev, follow), 0.0).astype(jnp.bfloat16)

    rank, count, templates = temporal_ref.shape
    blank = jnp.zeros((SLOT - count, templates), jnp.float32)
    for r in range(rank):
        value = jnp.concatenate([temporal_ref[r], blank], axis=0)
        high = value.astype(jnp.bfloat16).astype(jnp.float32)
        stacked = jnp.concatenate([high, high, value - high], axis=0)
        hat_ref[r] = jnp.dot(stacked.T.astype(jnp.bfloat16), spread_ref[...], preferred_element_type=jnp.float32)

    for main, sides, out in ((raw_ref, sides_ref, own_ref), (mate_ref, mate_sides_ref, near_ref)):
        count = main.shape[0]
        wide_ref[:count, :samples] = main[...]
        wide_ref[:count, samples:] = sides[...]
        out[...] = jnp.dot(wide_ref[:count], toep_ref[...], preferred_element_type=jnp.float32).astype(jnp.bfloat16)


def score_kernel(
    chunks,
    offsets_ref,
    toep_ref,
    far_ref,
    far_sides_ref,
    hat_ref,
    own_hbm,
    near_hbm,
    white_hbm,
    forward_hbm,
    inverse_hbm,
    spatial_hbm,
    keep_ref,
    send_ref,
    white_ref,
    forward_ref,
    inverse_ref,
    spatial_ref,
    wide_ref,
    filtered_ref,
    whitened_ref,
    what_ref,
    own_sem,
    near_sem,
    white_sem,
    forward_sem,
    inverse_sem,
    spatial_sem,
):
    rows, band = white_ref.shape
    samples = far_ref.shape[1]
    groups = offsets_ref.shape[0]
    tile = rows // groups
    c = lax.axis_index("chan")
    all_rows = lax.axis_size("chan") * rows
    rank, templates, _ = spatial_ref.shape
    block = templates // chunks
    even_core = c % 2 == 0
    near = pl.multiple_of(jnp.where(even_core, REACH + rows, 0), EDGE)
    far = pl.multiple_of(jnp.where(even_core, 0, REACH + rows), EDGE)

    own_copy = pltpu.make_async_copy(own_hbm, filtered_ref.at[REACH : REACH + rows], own_sem)
    near_copy = pltpu.make_async_copy(near_hbm, filtered_ref.at[pl.ds(near, REACH)], near_sem)
    white_copy = pltpu.make_async_copy(white_hbm, white_ref, white_sem)
    forward_copy = pltpu.make_async_copy(forward_hbm, forward_ref, forward_sem)
    inverse_copy = pltpu.make_async_copy(inverse_hbm, inverse_ref, inverse_sem)
    for copy in (own_copy, near_copy, white_copy, forward_copy):
        copy.start()
    later = []
    for chunk in range(chunks):
        part = (slice(None), slice(chunk * block, (chunk + 1) * block))
        later.append(pltpu.make_async_copy(spatial_hbm.at[part], spatial_ref.at[part], spatial_sem.at[chunk]))
        later[-1].start()
        if chunk == 0:
            inverse_copy.start()

    wide_ref[:, :samples] = far_ref[...]
    wide_ref[:, samples:] = far_sides_ref[...]
    value = jnp.dot(wide_ref[...], toep_ref[...], preferred_element_type=jnp.float32)
    filtered_ref[pl.ds(far, REACH)] = value.astype(jnp.bfloat16)

    own_copy.wait()
    near_copy.wait()
    white_copy.wait()
    for group in range(groups):
        begin = c * rows + group * tile
        start = begin + tile // 2 - band // 2 + offsets_ref[group] * tile
        start = jnp.clip(start, 0, all_rows - band) - c * rows + REACH
        start = pl.multiple_of(jnp.clip(start, 0, 2 * REACH + rows - band), EDGE)
        body = slice(group * tile, (group + 1) * tile)
        value = jnp.dot(white_ref[body], filtered_ref[pl.ds(start, band)], preferred_element_type=jnp.float32)
        whitened_ref[body] = value.astype(jnp.bfloat16)
    forward_copy.wait()
    value = jnp.dot(whitened_ref[...], forward_ref[0], preferred_element_type=jnp.float32)
    value += jnp.dot(whitened_ref[...], forward_ref[1], preferred_element_type=jnp.float32)
    what_ref[...] = value.astype(jnp.bfloat16)

    own = keep_ref.shape[1]
    inverse_copy.wait()
    for chunk in range(chunks):
        later[chunk].wait()
        body = slice(chunk * block, (chunk + 1) * block)
        weights = spatial_ref[:, body].reshape(rank * block, rows)
        product = jnp.dot(weights, what_ref[...], preferred_element_type=jnp.float32)
        real = imag = 0.0
        for r in range(rank):
            a = product[r * block : (r + 1) * block, :F]
            b = product[r * block : (r + 1) * block, F:]
            x = hat_ref[r, body, :F]
            y = hat_ref[r, body, F:]
            real += a * x + b * y
            imag += a * y - b * x
        both = jnp.concatenate([real, imag], axis=1).astype(jnp.bfloat16)
        value = jnp.dot(both, inverse_ref[0], preferred_element_type=jnp.float32)
        value += jnp.dot(both, inverse_ref[1], preferred_element_type=jnp.float32)
        pairs = block // (2 * own)
        for pair in range(pairs):
            even = value[2 * pair * own : (2 * pair + 1) * own]
            odd = value[(2 * pair + 1) * own : (2 * pair + 2) * own]
            keep_ref[chunk * pairs + pair] = jnp.where(even_core, even, odd)
            send_ref[chunk * pairs + pair] = jnp.where(even_core, odd, even).astype(jnp.bfloat16)


def couples(size):
    first = [(i, i ^ 1) for i in range(size)]
    second = [(i, ((i + 1) ^ 1) - 1) for i in range(1, size - 1)]
    return first, second


def local(raw, band_taps, whitening, band_offsets, spatial, temporal):
    rows, samples = raw.shape
    taps = band_taps.shape[0]
    band = whitening.shape[1]
    templates, rank, _ = spatial.shape
    window = samples + taps - 1
    n_tm = lax.axis_size("tm")
    n_chan = lax.axis_size("chan")
    own = templates // n_chan
    chunks = 2

    near_chan, far_chan = couples(n_chan)
    near_tm, far_tm = couples(n_tm)
    even_chan = lax.axis_index("chan") % 2 == 0
    vmem = pl.BlockSpec(memory_space=pltpu.VMEM)
    smem = pl.BlockSpec(memory_space=pltpu.SMEM)
    hbm = pl.BlockSpec(memory_space=pl.ANY)
    bf16 = jnp.bfloat16

    packed = jax.ShapeDtypeStruct((rows // 2, LANES), bf16)
    to_near, to_far = pl.pallas_call(
        pack_kernel,
        out_shape=(packed, packed),
        in_specs=[hbm],
        out_specs=(vmem, vmem),
        scratch_shapes=[pltpu.VMEM((2, rows, LANES), bf16), pltpu.SemaphoreType.DMA((2,))],
        cost_estimate=pl.CostEstimate(flops=rows * LANES, bytes_accessed=4 * rows * LANES, transcendentals=0),
        compiler_params=pltpu.CompilerParams(vmem_limit_bytes=4 << 20),
        name="pack",
    )(raw)
    first = lax.ppermute(to_near, "tm", near_tm)
    second = lax.ppermute(to_far, "tm", far_tm)
    facing = jax.ShapeDtypeStruct((REACH, samples), bf16)
    to_near, to_far = pl.pallas_call(
        face_kernel,
        out_shape=(facing, facing),
        in_specs=[hbm],
        out_specs=(vmem, vmem),
        scratch_shapes=[pltpu.SemaphoreType.DMA, pltpu.SemaphoreType.DMA],
        cost_estimate=pl.CostEstimate(flops=0, bytes_accessed=8 * REACH * samples, transcendentals=0),
        compiler_params=pltpu.CompilerParams(vmem_limit_bytes=2 << 20),
        name="face",
    )(raw)
    far = lax.ppermute(to_far, "chan", far_chan)
    near = lax.ppermute(to_near, "chan", near_chan)
    sides = jnp.concatenate(
        [
            jnp.concatenate([first[:, :EDGE], second[:, :EDGE]], axis=1),
            jnp.concatenate([first[:, EDGE:], second[:, EDGE:]], axis=1),
        ],
        axis=0,
    )
    upper, lower = sides[rows - REACH :], sides[:REACH]
    far_sides = lax.ppermute(jnp.where(even_chan, lower, upper), "chan", far_chan)
    near_sides = lax.ppermute(jnp.where(even_chan, upper, lower), "chan", near_chan)

    early = 2 * (rows + REACH) * WIDE * WIDE + 2 * rank * templates * 3 * SLOT * 2 * F
    toep, hat, own_rows, near_rows = pl.pallas_call(
        functools.partial(early_kernel, samples),
        out_shape=(
            jax.ShapeDtypeStruct((WIDE, WIDE), bf16),
            jax.ShapeDtypeStruct((rank, templates, 2 * F), jnp.float32),
            jax.ShapeDtypeStruct((rows, WIDE), bf16),
            jax.ShapeDtypeStruct((REACH, WIDE), bf16),
        ),
        in_specs=[vmem] * 7,
        out_specs=(vmem,) * 4,
        scratch_shapes=[pltpu.VMEM((rows, WIDE), bf16)],
        cost_estimate=pl.CostEstimate(flops=early, bytes_accessed=12 << 20, transcendentals=0),
        compiler_params=pltpu.CompilerParams(vmem_limit_bytes=24 << 20),
        name="early",
    )(band_taps[None], temporal.transpose(1, 2, 0), jnp.asarray(split_matrix(taps)), raw, sides, near, near_sides)
    forward = jnp.asarray(halves(forward_matrix(window, WIDE)))
    inverse = jnp.asarray(halves(inverse_matrix(samples)))

    out_shape = (n_chan // 2, own, samples)
    work = 2 * REACH * WIDE * WIDE + 2 * rows * WIDE * (band + 2 * WIDE) + 2 * templates * WIDE * (rank * rows + 2 * samples)
    keep, send = pl.pallas_call(
        functools.partial(score_kernel, chunks),
        out_shape=(
            jax.ShapeDtypeStruct(out_shape, jnp.float32),
            jax.ShapeDtypeStruct(out_shape, bf16),
        ),
        in_specs=[smem] + [vmem] * 4 + [hbm] * 6,
        out_specs=(vmem, vmem),
        scratch_shapes=[
            pltpu.VMEM((rows, band), bf16),
            pltpu.VMEM(forward.shape, bf16),
            pltpu.VMEM(inverse.shape, bf16),
            pltpu.VMEM((rank, templates, rows), bf16),
            pltpu.VMEM((REACH, WIDE), bf16),
            pltpu.VMEM((2 * REACH + rows, WIDE), bf16),
            pltpu.VMEM((rows, WIDE), bf16),
            pltpu.VMEM((rows, 2 * F), bf16),
            pltpu.SemaphoreType.DMA,
            pltpu.SemaphoreType.DMA,
            pltpu.SemaphoreType.DMA,
            pltpu.SemaphoreType.DMA,
            pltpu.SemaphoreType.DMA,
            pltpu.SemaphoreType.DMA((chunks,)),
        ],
        cost_estimate=pl.CostEstimate(flops=work, bytes_accessed=16 << 20, transcendentals=0),
        compiler_params=pltpu.CompilerParams(vmem_limit_bytes=36 << 20),
        name="score",
    )(band_offsets, toep, far, far_sides, hat, own_rows, near_rows, whitening, forward, inverse, spatial.transpose(1, 0, 2))

    other = lax.ppermute(send, "chan", near_chan)
    both = (keep + other.astype(jnp.float32)).astype(bf16)
    members = [[2 * i + core for i in range(n_chan // 2)] for core in range(2)]
    shares = lax.all_to_all(both, "chan", 0, 0, axis_index_groups=members)
    return jnp.sum(shares.astype(jnp.float32), axis=0)


def solution(mesh):
    placed = (P("chan", "tm"), P(), P("chan", None), P("chan"), P(None, None, "chan"), P())
    return jax.shard_map(local, mesh=mesh, in_specs=placed, out_specs=P("chan", "tm"), check_vma=False)
```

```python
import functools

import jax
import jax.numpy as jnp
import numpy as np
from jax import lax
from jax.experimental import pallas as pl
from jax.experimental.pallas import tpu as pltpu
from jax.sharding import PartitionSpec as P

LANES = 128
EDGE = 64
F = 256
POINTS = 2 * F - 1
WIDE = 512
SLOT = 64
REACH = 832


def halves(matrix):
    high = matrix.astype(jnp.bfloat16)
    low = (matrix - high.astype(np.float64)).astype(jnp.bfloat16)
    return np.stack([high, low])


def angles(samples):
    steps = np.outer(np.arange(samples), np.arange(F)) % POINTS
    return 2.0 * np.pi * steps / POINTS


def split_matrix(taps):
    high, low = halves(forward_matrix(taps, SLOT))
    return np.concatenate([high, low, high])


def forward_matrix(samples, rows):
    turn = angles(samples)
    full = np.zeros((rows, 2 * F))
    full[:samples] = np.concatenate([np.cos(turn), np.sin(turn)], axis=1)
    return full


def inverse_matrix(samples):
    turn = angles(samples).T
    weight = np.full((F, 1), 2.0 / POINTS)
    weight[0] = 1.0 / POINTS
    return np.concatenate([weight * np.cos(turn), -weight * np.sin(turn)], axis=0)


def pack(edge):
    half = edge.shape[0] // 2
    return jnp.concatenate([edge[:half], edge[half:]], axis=1)


def rolled(row, rows, shift):
    wide = jnp.broadcast_to(row, (rows, row.shape[1]))
    return pltpu.roll(wide, shift % row.shape[1], 1, stride=1, stride_axis=0)


def early_kernel(samples, taps_ref, temporal_ref, spread_ref, raw_ref, sides_ref, mate_ref, mate_sides_ref, toep_ref, hat_ref, own_ref, near_ref, wide_ref):
    taps = taps_ref.shape[1]
    t = lax.axis_index("tm")
    last = lax.axis_size("tm") - 1
    rest = (taps - 1) % 8
    reach = taps - 1 - rest
    tap = lax.broadcasted_iota(jnp.int32, (taps, WIDE), 0)
    lane = lax.broadcasted_iota(jnp.int32, (taps, WIDE), 1)
    place = (lane == rest - tap) | (lane == rest - tap + WIDE)
    picked = jnp.broadcast_to(taps_ref[...], (8, taps))
    row = jnp.dot(picked, place.astype(jnp.bfloat16), preferred_element_type=jnp.float32)[:1]
    begin = jnp.where(t == 0, taps // 2, 0)
    end = samples + jnp.where(t == last, taps // 2, taps - 1)
    column = lax.broadcasted_iota(jnp.int32, (1, WIDE), 1)
    keep = (column >= begin) & (column < end)
    prev = rolled(row, EDGE, reach - EDGE)
    follow = rolled(row, EDGE, reach + samples)
    even = t % 2 == 0
    toep_ref[:samples] = jnp.where(keep, rolled(row, samples, reach), 0.0).astype(jnp.bfloat16)
    toep_ref[samples : samples + EDGE] = jnp.where(keep, jnp.where(even, follow, prev), 0.0).astype(jnp.bfloat16)
    toep_ref[samples + EDGE :] = jnp.where(keep, jnp.where(even, prev, follow), 0.0).astype(jnp.bfloat16)

    rank, count, templates = temporal_ref.shape
    blank = jnp.zeros((SLOT - count, templates), jnp.float32)
    for r in range(rank):
        value = jnp.concatenate([temporal_ref[r], blank], axis=0)
        high = value.astype(jnp.bfloat16).astype(jnp.float32)
        stacked = jnp.concatenate([high, high, value - high], axis=0)
        hat_ref[r] = jnp.dot(stacked.T.astype(jnp.bfloat16), spread_ref[...], preferred_element_type=jnp.float32)

    for main, sides, out in ((raw_ref, sides_ref, own_ref), (mate_ref, mate_sides_ref, near_ref)):
        count = main.shape[0]
        wide_ref[:count, :samples] = main[...]
        wide_ref[:count, samples:] = sides[...]
        out[...] = jnp.dot(wide_ref[:count], toep_ref[...], preferred_element_type=jnp.float32).astype(jnp.bfloat16)


def score_kernel(
    chunks,
    offsets_ref,
    toep_ref,
    far_ref,
    far_sides_ref,
    hat_ref,
    own_hbm,
    near_hbm,
    white_hbm,
    forward_hbm,
    inverse_hbm,
    spatial_hbm,
    keep_ref,
    send_ref,
    white_ref,
    forward_ref,
    inverse_ref,
    spatial_ref,
    wide_ref,
    filtered_ref,
    whitened_ref,
    what_ref,
    own_sem,
    near_sem,
    white_sem,
    forward_sem,
    inverse_sem,
    spatial_sem,
):
    rows, band = white_ref.shape
    samples = far_ref.shape[1]
    groups = offsets_ref.shape[0]
    tile = rows // groups
    c = lax.axis_index("chan")
    all_rows = lax.axis_size("chan") * rows
    rank, templates, _ = spatial_ref.shape
    block = templates // chunks
    even_core = c % 2 == 0
    near = pl.multiple_of(jnp.where(even_core, REACH + rows, 0), EDGE)
    far = pl.multiple_of(jnp.where(even_core, 0, REACH + rows), EDGE)

    own_copy = pltpu.make_async_copy(own_hbm, filtered_ref.at[REACH : REACH + rows], own_sem)
    near_copy = pltpu.make_async_copy(near_hbm, filtered_ref.at[pl.ds(near, REACH)], near_sem)
    white_copy = pltpu.make_async_copy(white_hbm, white_ref, white_sem)
    forward_copy = pltpu.make_async_copy(forward_hbm, forward_ref, forward_sem)
    inverse_copy = pltpu.make_async_copy(inverse_hbm, inverse_ref, inverse_sem)
    for copy in (own_copy, near_copy, white_copy, forward_copy):
        copy.start()
    later = []
    for chunk in range(chunks):
        part = (slice(None), slice(chunk * block, (chunk + 1) * block))
        later.append(pltpu.make_async_copy(spatial_hbm.at[part], spatial_ref.at[part], spatial_sem.at[chunk]))
        later[-1].start()
        if chunk == 0:
            inverse_copy.start()

    wide_ref[:, :samples] = far_ref[...]
    wide_ref[:, samples:] = far_sides_ref[...]
    value = jnp.dot(wide_ref[...], toep_ref[...], preferred_element_type=jnp.float32)
    filtered_ref[pl.ds(far, REACH)] = value.astype(jnp.bfloat16)

    own_copy.wait()
    near_copy.wait()
    white_copy.wait()
    for group in range(groups):
        begin = c * rows + group * tile
        start = begin + tile // 2 - band // 2 + offsets_ref[group] * tile
        start = jnp.clip(start, 0, all_rows - band) - c * rows + REACH
        start = pl.multiple_of(jnp.clip(start, 0, 2 * REACH + rows - band), EDGE)
        body = slice(group * tile, (group + 1) * tile)
        value = jnp.dot(white_ref[body], filtered_ref[pl.ds(start, band)], preferred_element_type=jnp.float32)
        whitened_ref[body] = value.astype(jnp.bfloat16)
    forward_copy.wait()
    value = jnp.dot(whitened_ref[...], forward_ref[0], preferred_element_type=jnp.float32)
    value += jnp.dot(whitened_ref[...], forward_ref[1], preferred_element_type=jnp.float32)
    what_ref[...] = value.astype(jnp.bfloat16)

    own = keep_ref.shape[1]
    inverse_copy.wait()
    for chunk in range(chunks):
        later[chunk].wait()
        body = slice(chunk * block, (chunk + 1) * block)
        weights = spatial_ref[:, body].reshape(rank * block, rows)
        product = jnp.dot(weights, what_ref[...], preferred_element_type=jnp.float32)
        real = imag = 0.0
        for r in range(rank):
            a = product[r * block : (r + 1) * block, :F]
            b = product[r * block : (r + 1) * block, F:]
            x = hat_ref[r, body, :F]
            y = hat_ref[r, body, F:]
            real += a * x + b * y
            imag += a * y - b * x
        both = jnp.concatenate([real, imag], axis=1).astype(jnp.bfloat16)
        value = jnp.dot(both, inverse_ref[0], preferred_element_type=jnp.float32)
        value += jnp.dot(both, inverse_ref[1], preferred_element_type=jnp.float32)
        pairs = block // (2 * own)
        for pair in range(pairs):
            even = value[2 * pair * own : (2 * pair + 1) * own]
            odd = value[(2 * pair + 1) * own : (2 * pair + 2) * own]
            keep_ref[chunk * pairs + pair] = jnp.where(even_core, even, odd)
            send_ref[chunk * pairs + pair] = jnp.where(even_core, odd, even).astype(jnp.bfloat16)


def couples(size):
    first = [(i, i ^ 1) for i in range(size)]
    second = [(i, ((i + 1) ^ 1) - 1) for i in range(1, size - 1)]
    return first, second


def local(raw, band_taps, whitening, band_offsets, spatial, temporal):
    rows, samples = raw.shape
    taps = band_taps.shape[0]
    band = whitening.shape[1]
    templates, rank, _ = spatial.shape
    window = samples + taps - 1
    n_tm = lax.axis_size("tm")
    n_chan = lax.axis_size("chan")
    own = templates // n_chan
    chunks = 2

    near_chan, far_chan = couples(n_chan)
    near_tm, far_tm = couples(n_tm)
    even_tm = lax.axis_index("tm") % 2 == 0
    even_chan = lax.axis_index("chan") % 2 == 0

    def facing(array):
        upper, lower = array[rows - REACH :], array[:REACH]
        return jnp.where(even_chan, upper, lower), jnp.where(even_chan, lower, upper)

    to_near, to_far = facing(raw)
    far = lax.ppermute(to_far, "chan", far_chan)
    near = lax.ppermute(to_near, "chan", near_chan)
    ahead, behind = pack(raw[:, samples - EDGE :]), pack(raw[:, :EDGE])
    to_second = jnp.where(even_tm, behind, ahead)
    to_second, near = lax.optimization_barrier((to_second, near))
    first = lax.ppermute(jnp.where(even_tm, ahead, behind), "tm", near_tm)
    second = lax.ppermute(to_second, "tm", far_tm)
    sides = jnp.concatenate(
        [
            jnp.concatenate([first[:, :EDGE], second[:, :EDGE]], axis=1),
            jnp.concatenate([first[:, EDGE:], second[:, EDGE:]], axis=1),
        ],
        axis=0,
    )
    to_near, to_far = facing(sides)
    far_sides = lax.ppermute(to_far, "chan", far_chan)
    near_sides = lax.ppermute(to_near, "chan", near_chan)

    vmem = pl.BlockSpec(memory_space=pltpu.VMEM)
    smem = pl.BlockSpec(memory_space=pltpu.SMEM)
    hbm = pl.BlockSpec(memory_space=pl.ANY)
    bf16 = jnp.bfloat16
    toep, hat, own_rows, near_rows = pl.pallas_call(
        functools.partial(early_kernel, samples),
        out_shape=(
            jax.ShapeDtypeStruct((WIDE, WIDE), bf16),
            jax.ShapeDtypeStruct((rank, templates, 2 * F), jnp.float32),
            jax.ShapeDtypeStruct((rows, WIDE), bf16),
            jax.ShapeDtypeStruct((REACH, WIDE), bf16),
        ),
        in_specs=[vmem] * 7,
        out_specs=(vmem,) * 4,
        scratch_shapes=[pltpu.VMEM((rows, WIDE), bf16)],
        cost_estimate=pl.CostEstimate(flops=1024, bytes_accessed=1024, transcendentals=0),
        compiler_params=pltpu.CompilerParams(vmem_limit_bytes=24 << 20),
        name="early",
    )(band_taps[None], temporal.transpose(1, 2, 0), jnp.asarray(split_matrix(taps)), raw, sides, near, near_sides)
    forward = jnp.asarray(halves(forward_matrix(window, WIDE)))
    inverse = jnp.asarray(halves(inverse_matrix(samples)))

    out_shape = (n_chan // 2, own, samples)
    work = 2 * REACH * WIDE * WIDE + 2 * rows * WIDE * (band + 2 * WIDE) + 2 * templates * WIDE * (rank * rows + 2 * samples)
    keep, send = pl.pallas_call(
        functools.partial(score_kernel, chunks),
        out_shape=(
            jax.ShapeDtypeStruct(out_shape, jnp.float32),
            jax.ShapeDtypeStruct(out_shape, bf16),
        ),
        in_specs=[smem] + [vmem] * 4 + [hbm] * 6,
        out_specs=(vmem, vmem),
        scratch_shapes=[
            pltpu.VMEM((rows, band), bf16),
            pltpu.VMEM(forward.shape, bf16),
            pltpu.VMEM(inverse.shape, bf16),
            pltpu.VMEM((rank, templates, rows), bf16),
            pltpu.VMEM((REACH, WIDE), bf16),
            pltpu.VMEM((2 * REACH + rows, WIDE), bf16),
            pltpu.VMEM((rows, WIDE), bf16),
            pltpu.VMEM((rows, 2 * F), bf16),
            pltpu.SemaphoreType.DMA,
            pltpu.SemaphoreType.DMA,
            pltpu.SemaphoreType.DMA,
            pltpu.SemaphoreType.DMA,
            pltpu.SemaphoreType.DMA,
            pltpu.SemaphoreType.DMA((chunks,)),
        ],
        cost_estimate=pl.CostEstimate(flops=work, bytes_accessed=16 << 20, transcendentals=0),
        compiler_params=pltpu.CompilerParams(vmem_limit_bytes=36 << 20),
        name="score",
    )(band_offsets, toep, far, far_sides, hat, own_rows, near_rows, whitening, forward, inverse, spatial.transpose(1, 0, 2))

    other = lax.ppermute(send, "chan", near_chan)
    both = (keep + other.astype(jnp.float32)).astype(bf16)
    members = [[2 * i + core for i in range(n_chan // 2)] for core in range(2)]
    shares = lax.all_to_all(both, "chan", 0, 0, axis_index_groups=members)
    return jnp.sum(shares.astype(jnp.float32), axis=0)


def solution(mesh):
    placed = (P("chan", "tm"), P(), P("chan", None), P("chan"), P(None, None, "chan"), P())
    return jax.shard_map(local, mesh=mesh, in_specs=placed, out_specs=P("chan", "tm"), check_vma=False)
```

```python
import functools

import jax
import jax.numpy as jnp
import numpy as np
from jax import lax
from jax.experimental import pallas as pl
from jax.experimental.pallas import tpu as pltpu
from jax.sharding import PartitionSpec as P

LANES = 128
EDGE = 64
F = 256
POINTS = 2 * F - 1
WIDE = 512
SLOT = 64
REACH = 832


def halves(matrix):
    high = matrix.astype(jnp.bfloat16)
    low = (matrix - high.astype(np.float64)).astype(jnp.bfloat16)
    return np.stack([high, low])


def angles(samples):
    steps = np.outer(np.arange(samples), np.arange(F)) % POINTS
    return 2.0 * np.pi * steps / POINTS


def split_matrix(taps):
    high, low = halves(forward_matrix(taps, SLOT))
    return np.concatenate([high, low, high])


def forward_matrix(samples, rows):
    turn = angles(samples)
    full = np.zeros((rows, 2 * F))
    full[:samples] = np.concatenate([np.cos(turn), np.sin(turn)], axis=1)
    return full


def inverse_matrix(samples):
    turn = angles(samples).T
    weight = np.full((F, 1), 2.0 / POINTS)
    weight[0] = 1.0 / POINTS
    return np.concatenate([weight * np.cos(turn), -weight * np.sin(turn)], axis=0)


def pack(edge):
    half = edge.shape[0] // 2
    return jnp.concatenate([edge[:half], edge[half:]], axis=1)


def rolled(row, rows, shift):
    wide = jnp.broadcast_to(row, (rows, row.shape[1]))
    return pltpu.roll(wide, shift % row.shape[1], 1, stride=1, stride_axis=0)


def early_kernel(samples, taps_ref, temporal_ref, spread_ref, raw_ref, sides_ref, mate_ref, mate_sides_ref, toep_ref, hat_ref, own_ref, near_ref, wide_ref):
    taps = taps_ref.shape[1]
    t = lax.axis_index("tm")
    last = lax.axis_size("tm") - 1
    rest = (taps - 1) % 8
    reach = taps - 1 - rest
    tap = lax.broadcasted_iota(jnp.int32, (taps, WIDE), 0)
    lane = lax.broadcasted_iota(jnp.int32, (taps, WIDE), 1)
    place = (lane == rest - tap) | (lane == rest - tap + WIDE)
    picked = jnp.broadcast_to(taps_ref[...], (8, taps))
    row = jnp.dot(picked, place.astype(jnp.bfloat16), preferred_element_type=jnp.float32)[:1]
    begin = jnp.where(t == 0, taps // 2, 0)
    end = samples + jnp.where(t == last, taps // 2, taps - 1)
    column = lax.broadcasted_iota(jnp.int32, (1, WIDE), 1)
    keep = (column >= begin) & (column < end)
    prev = rolled(row, EDGE, reach - EDGE)
    follow = rolled(row, EDGE, reach + samples)
    even = t % 2 == 0
    toep_ref[:samples] = jnp.where(keep, rolled(row, samples, reach), 0.0).astype(jnp.bfloat16)
    toep_ref[samples : samples + EDGE] = jnp.where(keep, jnp.where(even, follow, prev), 0.0).astype(jnp.bfloat16)
    toep_ref[samples + EDGE :] = jnp.where(keep, jnp.where(even, prev, follow), 0.0).astype(jnp.bfloat16)

    rank, count, templates = temporal_ref.shape
    blank = jnp.zeros((SLOT - count, templates), jnp.float32)
    for r in range(rank):
        value = jnp.concatenate([temporal_ref[r], blank], axis=0)
        high = value.astype(jnp.bfloat16).astype(jnp.float32)
        stacked = jnp.concatenate([high, high, value - high], axis=0)
        hat_ref[r] = jnp.dot(stacked.T.astype(jnp.bfloat16), spread_ref[...], preferred_element_type=jnp.float32)

    for main, sides, out in ((raw_ref, sides_ref, own_ref), (mate_ref, mate_sides_ref, near_ref)):
        count = main.shape[0]
        wide_ref[:count, :samples] = main[...]
        wide_ref[:count, samples:] = sides[...]
        out[...] = jnp.dot(wide_ref[:count], toep_ref[...], preferred_element_type=jnp.float32).astype(jnp.bfloat16)


def score_kernel(
    chunks,
    offsets_ref,
    toep_ref,
    far_ref,
    far_sides_ref,
    hat_ref,
    own_hbm,
    near_hbm,
    white_hbm,
    forward_hbm,
    inverse_hbm,
    spatial_hbm,
    keep_ref,
    send_ref,
    white_ref,
    forward_ref,
    inverse_ref,
    spatial_ref,
    wide_ref,
    filtered_ref,
    whitened_ref,
    what_ref,
    own_sem,
    near_sem,
    white_sem,
    forward_sem,
    inverse_sem,
    spatial_sem,
):
    rows, band = white_ref.shape
    samples = far_ref.shape[1]
    groups = offsets_ref.shape[0]
    tile = rows // groups
    c = lax.axis_index("chan")
    all_rows = lax.axis_size("chan") * rows
    rank, templates, _ = spatial_ref.shape
    block = templates // chunks
    even_core = c % 2 == 0
    near = pl.multiple_of(jnp.where(even_core, REACH + rows, 0), EDGE)
    far = pl.multiple_of(jnp.where(even_core, 0, REACH + rows), EDGE)

    own_copy = pltpu.make_async_copy(own_hbm, filtered_ref.at[REACH : REACH + rows], own_sem)
    near_copy = pltpu.make_async_copy(near_hbm, filtered_ref.at[pl.ds(near, REACH)], near_sem)
    white_copy = pltpu.make_async_copy(white_hbm, white_ref, white_sem)
    forward_copy = pltpu.make_async_copy(forward_hbm, forward_ref, forward_sem)
    inverse_copy = pltpu.make_async_copy(inverse_hbm, inverse_ref, inverse_sem)
    for copy in (own_copy, near_copy, white_copy, forward_copy):
        copy.start()
    later = []
    for chunk in range(chunks):
        part = (slice(None), slice(chunk * block, (chunk + 1) * block))
        later.append(pltpu.make_async_copy(spatial_hbm.at[part], spatial_ref.at[part], spatial_sem.at[chunk]))
        later[-1].start()
        if chunk == 0:
            inverse_copy.start()

    wide_ref[:, :samples] = far_ref[...]
    wide_ref[:, samples:] = far_sides_ref[...]
    value = jnp.dot(wide_ref[...], toep_ref[...], preferred_element_type=jnp.float32)
    filtered_ref[pl.ds(far, REACH)] = value.astype(jnp.bfloat16)

    own_copy.wait()
    near_copy.wait()
    white_copy.wait()
    for group in range(groups):
        begin = c * rows + group * tile
        start = begin + tile // 2 - band // 2 + offsets_ref[group] * tile
        start = jnp.clip(start, 0, all_rows - band) - c * rows + REACH
        start = pl.multiple_of(jnp.clip(start, 0, 2 * REACH + rows - band), EDGE)
        body = slice(group * tile, (group + 1) * tile)
        value = jnp.dot(white_ref[body], filtered_ref[pl.ds(start, band)], preferred_element_type=jnp.float32)
        whitened_ref[body] = value.astype(jnp.bfloat16)
    forward_copy.wait()
    value = jnp.dot(whitened_ref[...], forward_ref[0], preferred_element_type=jnp.float32)
    value += jnp.dot(whitened_ref[...], forward_ref[1], preferred_element_type=jnp.float32)
    what_ref[...] = value.astype(jnp.bfloat16)

    own = keep_ref.shape[1]
    inverse_copy.wait()
    for chunk in range(chunks):
        later[chunk].wait()
        body = slice(chunk * block, (chunk + 1) * block)
        weights = spatial_ref[:, body].reshape(rank * block, rows)
        product = jnp.dot(weights, what_ref[...], preferred_element_type=jnp.float32)
        real = imag = 0.0
        for r in range(rank):
            a = product[r * block : (r + 1) * block, :F]
            b = product[r * block : (r + 1) * block, F:]
            x = hat_ref[r, body, :F]
            y = hat_ref[r, body, F:]
            real += a * x + b * y
            imag += a * y - b * x
        both = jnp.concatenate([real, imag], axis=1).astype(jnp.bfloat16)
        value = jnp.dot(both, inverse_ref[0], preferred_element_type=jnp.float32)
        value += jnp.dot(both, inverse_ref[1], preferred_element_type=jnp.float32)
        pairs = block // (2 * own)
        for pair in range(pairs):
            even = value[2 * pair * own : (2 * pair + 1) * own]
            odd = value[(2 * pair + 1) * own : (2 * pair + 2) * own]
            keep_ref[chunk * pairs + pair] = jnp.where(even_core, even, odd)
            send_ref[chunk * pairs + pair] = jnp.where(even_core, odd, even).astype(jnp.bfloat16)


def couples(size):
    first = [(i, i ^ 1) for i in range(size)]
    second = [(i, ((i + 1) ^ 1) - 1) for i in range(1, size - 1)]
    return first, second


def local(raw, band_taps, whitening, band_offsets, spatial, temporal):
    rows, samples = raw.shape
    taps = band_taps.shape[0]
    band = whitening.shape[1]
    templates, rank, _ = spatial.shape
    window = samples + taps - 1
    n_tm = lax.axis_size("tm")
    n_chan = lax.axis_size("chan")
    own = templates // n_chan
    chunks = 1

    near_chan, far_chan = couples(n_chan)
    near_tm, far_tm = couples(n_tm)
    even_tm = lax.axis_index("tm") % 2 == 0
    even_chan = lax.axis_index("chan") % 2 == 0

    def facing(array):
        upper, lower = array[rows - REACH :], array[:REACH]
        return jnp.where(even_chan, upper, lower), jnp.where(even_chan, lower, upper)

    ahead, behind = pack(raw[:, samples - EDGE :]), pack(raw[:, :EDGE])
    first = lax.ppermute(jnp.where(even_tm, ahead, behind), "tm", near_tm)
    second = lax.ppermute(jnp.where(even_tm, behind, ahead), "tm", far_tm)
    upper = rows - REACH
    to_far = lax.dynamic_slice_in_dim(raw, jnp.where(even_chan, 0, upper), REACH, 0)
    to_near = lax.dynamic_slice_in_dim(raw, jnp.where(even_chan, upper, 0), REACH, 0)
    far = lax.ppermute(to_far, "chan", far_chan)
    near = lax.ppermute(to_near, "chan", near_chan)
    sides = jnp.concatenate(
        [
            jnp.concatenate([first[:, :EDGE], second[:, :EDGE]], axis=1),
            jnp.concatenate([first[:, EDGE:], second[:, EDGE:]], axis=1),
        ],
        axis=0,
    )
    to_near, to_far = facing(sides)
    far_sides = lax.ppermute(to_far, "chan", far_chan)
    near_sides = lax.ppermute(to_near, "chan", near_chan)

    vmem = pl.BlockSpec(memory_space=pltpu.VMEM)
    smem = pl.BlockSpec(memory_space=pltpu.SMEM)
    hbm = pl.BlockSpec(memory_space=pl.ANY)
    bf16 = jnp.bfloat16
    toep, hat, own_rows, near_rows = pl.pallas_call(
        functools.partial(early_kernel, samples),
        out_shape=(
            jax.ShapeDtypeStruct((WIDE, WIDE), bf16),
            jax.ShapeDtypeStruct((rank, templates, 2 * F), jnp.float32),
            jax.ShapeDtypeStruct((rows, WIDE), bf16),
            jax.ShapeDtypeStruct((REACH, WIDE), bf16),
        ),
        in_specs=[vmem] * 7,
        out_specs=(vmem,) * 4,
        scratch_shapes=[pltpu.VMEM((rows, WIDE), bf16)],
        cost_estimate=pl.CostEstimate(flops=1024, bytes_accessed=1024, transcendentals=0),
        compiler_params=pltpu.CompilerParams(vmem_limit_bytes=24 << 20),
        name="early",
    )(band_taps[None], temporal.transpose(1, 2, 0), jnp.asarray(split_matrix(taps)), raw, sides, near, near_sides)
    forward = jnp.asarray(halves(forward_matrix(window, WIDE)))
    inverse = jnp.asarray(halves(inverse_matrix(samples)))

    out_shape = (n_chan // 2, own, samples)
    work = 2 * REACH * WIDE * WIDE + 2 * rows * WIDE * (band + 2 * WIDE) + 2 * templates * WIDE * (rank * rows + 2 * samples)
    keep, send = pl.pallas_call(
        functools.partial(score_kernel, chunks),
        out_shape=(
            jax.ShapeDtypeStruct(out_shape, jnp.float32),
            jax.ShapeDtypeStruct(out_shape, bf16),
        ),
        in_specs=[smem] + [vmem] * 4 + [hbm] * 6,
        out_specs=(vmem, vmem),
        scratch_shapes=[
            pltpu.VMEM((rows, band), bf16),
            pltpu.VMEM(forward.shape, bf16),
            pltpu.VMEM(inverse.shape, bf16),
            pltpu.VMEM((rank, templates, rows), bf16),
            pltpu.VMEM((REACH, WIDE), bf16),
            pltpu.VMEM((2 * REACH + rows, WIDE), bf16),
            pltpu.VMEM((rows, WIDE), bf16),
            pltpu.VMEM((rows, 2 * F), bf16),
            pltpu.SemaphoreType.DMA,
            pltpu.SemaphoreType.DMA,
            pltpu.SemaphoreType.DMA,
            pltpu.SemaphoreType.DMA,
            pltpu.SemaphoreType.DMA,
            pltpu.SemaphoreType.DMA((chunks,)),
        ],
        cost_estimate=pl.CostEstimate(flops=work, bytes_accessed=16 << 20, transcendentals=0),
        compiler_params=pltpu.CompilerParams(vmem_limit_bytes=36 << 20),
        name="score",
    )(band_offsets, toep, far, far_sides, hat, own_rows, near_rows, whitening, forward, inverse, spatial.transpose(1, 0, 2))

    other = lax.ppermute(send, "chan", near_chan)
    both = (keep + other.astype(jnp.float32)).astype(bf16)
    members = [[2 * i + core for i in range(n_chan // 2)] for core in range(2)]
    shares = lax.all_to_all(both, "chan", 0, 0, axis_index_groups=members)
    return jnp.sum(shares.astype(jnp.float32), axis=0)


def solution(mesh):
    placed = (P("chan", "tm"), P(), P("chan", None), P("chan"), P(None, None, "chan"), P())
    return jax.shard_map(local, mesh=mesh, in_specs=placed, out_specs=P("chan", "tm"), check_vma=False)
```
